32 devices in a mesh: dp: 4 (over x, core), fsdp: 8 (over z, y).
Axes of the slice: x: 2, y: 2, z: 4, core: 2. Of those that a mesh axis runs over, the one named last changes fastest.
Arguments:
- tokens: bfloat16 [32768, 1024], P(('dp', 'fsdp')), may hold values from -6 to 6
- first_values: bfloat16 [32768, 1024], P(('dp', 'fsdp')), may hold values from -6 to 6
- cotangent: bfloat16 [32768, 1024], P(('dp', 'fsdp')), may hold values from -6 to 6
- lengths: int32 [64, 8], P(('dp', 'fsdp')), may hold values from 0 to 512, as said below
- w_query: bfloat16 [1024, 1024], P(('dp', 'fsdp')), may hold values from -0.1875 to 0.1875
- w_key: bfloat16 [1024, 1024], P(('dp', 'fsdp')), may hold values from -0.1875 to 0.1875
- w_value: bfloat16 [1024, 1024], P(('dp', 'fsdp')), may hold values from -0.1875 to 0.1875
- w_out: bfloat16 [1024, 1024], P(('dp', 'fsdp')), may hold values from -0.75 to 0.75
- w_gate: bfloat16 [1024, 2816], P(('dp', 'fsdp')), may hold values from -0.1875 to 0.1875
- w_up: bfloat16 [1024, 2816], P(('dp', 'fsdp')), may hold values from -0.1875 to 0.1875
- w_down: bfloat16 [2816, 1024], P(('dp', 'fsdp')), may hold values from -0.109375 to 0.109375
- gain_one: bfloat16 [1024], P(('dp', 'fsdp')), may hold values from 0.5 to 1.5
- gain_two: bfloat16 [1024], P(('dp', 'fsdp')), may hold values from 0.5 to 1.5
Outputs:
- out_tokens: bfloat16 [32768, 1024], P(('dp', 'fsdp'))
- grad_tokens: float32 [32768, 1024], P(('dp', 'fsdp'))
- grad_first_values: float32 [32768, 1024], P(('dp', 'fsdp'))
- grad_query: float32 [1024, 1024], P(('dp', 'fsdp'))
- grad_key: float32 [1024, 1024], P(('dp', 'fsdp'))
- grad_value: float32 [1024, 1024], P(('dp', 'fsdp'))
- grad_out: float32 [1024, 1024], P(('dp', 'fsdp'))
- grad_gate: float32 [1024, 2816], P(('dp', 'fsdp'))
- grad_up: float32 [1024, 2816], P(('dp', 'fsdp'))
- grad_down: float32 [2816, 1024], P(('dp', 'fsdp'))
- grad_gain_one: float32 [1024], P(('dp', 'fsdp'))
- grad_gain_two: float32 [1024], P(('dp', 'fsdp'))
The draws below stay inside these ranges and needn't reach their ends.
Inputs may be any that keep to these rules, and one draw needn't show every extreme that they name: Row b lists the lengths of the sequences of bucket b, laid one after another from the bucket's first slot; 0 marks no sequence; a row adds up to at most 512, and the slots after its total are padding; bucket 0 holds one sequence of 512 tokens. Bucket b is micro-batch b % 2 of the device that holds its slots.
All inputs are finite; a program needn't handle non-finite values.
Results may differ from the reference program's by a relative error of at most 0.014.
Values may be sent and summed in bfloat16 or wider, within the bound.
No kernel may reach another device: no remote copies, remote signals or barrier semaphores. Data moves between devices by JAX's collectives and lax.ppermute only.
A program may use at most 256 MiB of HBM per device.

```python
import math
from functools import partial
import jax
import jax.numpy as jnp
from jax import lax

D = 1024
HEADS = 16
HEAD_DIM = 64
FF = 2816
SLOTS = 512
NSEQ = 8
BUCKETS = 64
TOKENS = 32768


def draw_lengths(key, part):
    key_shift, key_jitter = jax.random.split(key)
    shifts = jax.random.randint(key_shift, (BUCKETS, NSEQ), 0, 4)
    base_length = jnp.int32(SLOTS) // jnp.left_shift(jnp.int32(1), shifts)
    jitter = jax.random.randint(key_jitter, (BUCKETS, NSEQ), 0, 1 << 20) % (base_length // 2 + 1)
    candidate = jnp.minimum(base_length + jitter, SLOTS).astype(jnp.int32)

    def pack_step(used_slots, next_column):
        taken_rows = jnp.where(used_slots + next_column <= SLOTS, next_column, 0)
        return (used_slots + taken_rows, taken_rows)
    used_slots, taken_rows = lax.scan(pack_step, jnp.zeros((BUCKETS,), jnp.int32), candidate.T)
    packed = taken_rows.T
    first_row = jnp.zeros((NSEQ,), jnp.int32).at[0].set(SLOTS)
    bucket_index = jnp.arange(BUCKETS)[:, None]
    return jnp.where(bucket_index == 0, first_row[None, :], packed).astype(jnp.int32)


def shard_levels(stream_key, dims, cuts, low, top_value):
    def one(dim, blocks):
        heights = jax.random.uniform(jax.random.fold_in(jax.random.fold_in(stream_key, 6), dim), (blocks,), jnp.float32, low / len(cuts), top_value / len(cuts))
        return jnp.repeat(jnp.exp(heights), dims[dim] // blocks).reshape((-1,) + (1,) * (len(dims) - dim - 1))

    gain = one(*cuts[0])
    for cut in cuts[1:]:
        gain = gain * one(*cut)
    return gain


def noise(rng, extent, width, bound, pieces=(), held_as=jnp.bfloat16):
    gain = shard_levels(rng, extent, pieces, -0.22, 0.18) if pieces else 1.0
    array = jax.random.normal(rng, extent, jnp.float32) * width * gain
    return jnp.minimum(jnp.maximum(array, -bound), bound).astype(held_as)


def setup_inputs(seed: int = 0) -> dict:
    splits = jax.random.split(jax.random.key(seed), 14)
    return {
        "tokens": noise(splits[0], (TOKENS, D), 1.0, 6.0, ((0, 32),)),
        "first_values": noise(splits[1], (TOKENS, D), 1.0, 6.0, ((0, 32),)),
        "cotangent": noise(splits[2], (TOKENS, D), 1.0, 6.0, ((0, 32),)),
        "lengths": draw_lengths(jax.random.fold_in(splits[13], 71), 0),
        "w_query": noise(splits[4], (D, D), D ** -0.5, 0.1875, ((0, 32),)),
        "w_key": noise(splits[5], (D, D), D ** -0.5, 0.1875, ((0, 32),)),
        "w_value": noise(splits[6], (D, D), D ** -0.5, 0.1875, ((0, 32),)),
        "w_out": noise(splits[7], (D, D), (D // 16) ** -0.5, 0.75, ((0, 32),)),
        "w_gate": noise(splits[8], (D, FF), D ** -0.5, 0.1875, ((0, 32),)),
        "w_up": noise(splits[9], (D, FF), D ** -0.5, 0.1875, ((0, 32),)),
        "w_down": noise(splits[10], (FF, D), FF ** -0.5, 0.109375, ((0, 32),)),
        "gain_one": jnp.clip(1.0 + 0.1 * jax.random.normal(splits[11], (D,), jnp.float32), 0.5, 1.5).astype(jnp.bfloat16),
        "gain_two": jnp.clip(1.0 + 0.1 * jax.random.normal(splits[12], (D,), jnp.float32), 0.5, 1.5).astype(jnp.bfloat16),
    }


@jax.custom_vjp
def low(v):
    return lax.optimization_barrier(v.astype(jnp.bfloat16)).astype(jnp.float32)

@jax.custom_vjp
def low_back(v):
    return v

def low_keep(v):
    return (low(v), None)

def low_pass(kept, grad):
    return (grad,)

def back_keep(v):
    return (v, None)

def back_low(kept, grad):
    return (low(grad),)
low.defvjp(low_keep, low_pass)
low_back.defvjp(back_keep, back_low)
EPSILON = 1e-06
HIGHEST = lax.Precision.HIGHEST

def matmul(left, right):
    return jnp.dot(left, right, precision=HIGHEST)

def bucket_layout(lengths_row, slot_count):
    seq_ends = jnp.cumsum(lengths_row).astype(jnp.int32)
    slot_places = jnp.arange(slot_count, dtype=jnp.int32)
    ended_mask = seq_ends[None, :] <= slot_places[:, None]
    segment = lax.optimization_barrier(jnp.sum(ended_mask.astype(jnp.int32), axis=1))
    before_total = lax.optimization_barrier(jnp.sum(jnp.where(ended_mask, lengths_row[None, :], 0), axis=1)).astype(jnp.int32)
    return (segment, slot_places - before_total, slot_places < seq_ends[-1])

def rope_tables(position, head_size):
    half_size = head_size // 2
    frequency = jnp.exp(jnp.arange(half_size, dtype=jnp.float32) * (-2.0 * math.log(10000.0) / head_size))
    angles = position.astype(jnp.float32)[:, None] * frequency[None, :]
    return (jnp.cos(angles), jnp.sin(angles))

def rotate(matrix, cosine, sine, head_count):
    row_count = matrix.shape[0]
    halves = matrix.reshape(row_count, head_count, 2, -1)
    first_half = halves[:, :, 0]
    second_half = halves[:, :, 1]
    cos_table = cosine[:, None, :]
    sin_table = sine[:, None, :]
    turned = jnp.stack([first_half * cos_table - second_half * sin_table, second_half * cos_table + first_half * sin_table], axis=2)
    return turned.reshape(row_count, -1)

def allowed_mask(segment, valid):
    slot_places = jnp.arange(segment.shape[0])
    earlier = slot_places[None, :] < slot_places[:, None]
    same_seq = segment[:, None] == segment[None, :]
    diagonal = slot_places[None, :] == slot_places[:, None]
    return diagonal | same_seq & earlier & valid[:, None]

def rms_scale(matrix):
    return lax.rsqrt(lax.optimization_barrier(jnp.mean(matrix * matrix, axis=-1, keepdims=True)) + EPSILON)

def attend_bucket(block):
    query_rot, key_rot, value_mix, segment, valid = block
    slot_count = query_rot.shape[0]
    query_heads = query_rot.reshape(slot_count, HEADS, HEAD_DIM)
    key_heads = key_rot.reshape(slot_count, HEADS, HEAD_DIM)
    value_heads = value_mix.reshape(slot_count, HEADS, HEAD_DIM)
    scores = jnp.einsum('qhd,khd->hqk', query_heads, key_heads, precision=HIGHEST) * HEAD_DIM ** (-0.5)
    scores = low_back(scores)
    scores = jnp.where(allowed_mask(segment, valid)[None], scores, -1e+30)
    probs = low(jax.nn.softmax(scores, axis=-1))
    mixed_heads = jnp.einsum('hqk,khd->qhd', probs, value_heads, precision=HIGHEST)
    return mixed_heads.reshape(slot_count, -1)

def layer(inputs, first_input, w_query, w_key, w_value, w_out, w_gate, w_up, w_down, gain_one, gain_two, cosine, sine, segment, valid):
    groups, slot_count = segment.shape
    model_width = inputs.shape[1]
    normed = low(inputs * rms_scale(inputs) * gain_one)
    query_rot = low(rotate(low_back(matmul(normed, w_query)), cosine, sine, HEADS))
    key_rot = low(rotate(low_back(matmul(normed, w_key)), cosine, sine, HEADS))
    value_mix = low(0.5 * low_back(matmul(normed, w_value)) + 0.5 * first_input)
    mixed_heads = lax.map(jax.checkpoint(attend_bucket), (query_rot.reshape(groups, slot_count, model_width), key_rot.reshape(groups, slot_count, model_width), value_mix.reshape(groups, slot_count, model_width), segment, valid))
    context = low(low_back(mixed_heads.reshape(groups * slot_count, model_width)))
    hidden = inputs + low_back(matmul(context, w_out))
    normed_two = low(hidden * rms_scale(hidden) * gain_two)
    gate_values = low_back(matmul(normed_two, w_gate))
    upward = low_back(matmul(normed_two, w_up))
    product = low(jax.nn.silu(gate_values) * upward)
    return hidden + low_back(matmul(product, w_down))

def reference(tokens, first_values, cotangent, lengths, w_query, w_key, w_value, w_out, w_gate, w_up, w_down, gain_one, gain_two):
    params = tuple((member.astype(jnp.float32) for member in (w_query, w_key, w_value, w_out, w_gate, w_up, w_down, gain_one, gain_two)))
    segment, position, valid = jax.vmap(partial(bucket_layout, slot_count=SLOTS))(lengths)
    group_size = 4 if BUCKETS % 4 == 0 else 1
    block_count = BUCKETS // group_size
    half_size = HEAD_DIM // 2
    cosine, sine = rope_tables(position.reshape(-1), HEAD_DIM)
    valid_rows = valid.reshape(-1).astype(jnp.float32)[:, None]
    scan_inputs = (tokens.astype(jnp.float32).reshape(block_count, group_size * SLOTS, D), first_values.astype(jnp.float32).reshape(block_count, group_size * SLOTS, D), (cotangent.astype(jnp.float32) * valid_rows).reshape(block_count, group_size * SLOTS, D), cosine.reshape(block_count, group_size * SLOTS, half_size), sine.reshape(block_count, group_size * SLOTS, half_size), segment.reshape(block_count, group_size, SLOTS), valid.reshape(block_count, group_size, SLOTS))

    def scan_step(totals, block):
        block_tokens, block_first, block_cotangent, block_cos, block_sin, block_segment, block_valid = block

        def forward(inputs, first_input, *weight_set):
            return layer(inputs, first_input, *weight_set, block_cos, block_sin, block_segment, block_valid)
        outputs, pullback = jax.vjp(forward, block_tokens, block_first, *params)
        gradients = pullback(block_cotangent)
        new_totals = tuple((running_total + new_grad for running_total, new_grad in zip(totals, gradients[2:])))
        return (new_totals, (outputs.astype(jnp.bfloat16), gradients[0], gradients[1]))
    zero_totals = tuple((jnp.zeros_like(member) for member in params))
    totals, scanned = lax.scan(scan_step, zero_totals, scan_inputs)
    return (scanned[0].reshape(TOKENS, D), scanned[1].reshape(TOKENS, D), scanned[2].reshape(TOKENS, D), totals[0], totals[1], totals[2], totals[3], totals[4], totals[5], totals[6], totals[7], totals[8])
```

```python
import math
from functools import partial

import jax
import jax.numpy as jnp
from jax import lax
from jax.sharding import PartitionSpec as P

HEADS = 16


EPSILON = 1e-06


def forward_dot(left, right):
    return jnp.dot(left, right, preferred_element_type=jnp.float32)


def contract_last(left, right):
    return lax.dot_general(
        left, right, (((1,), (1,)), ((), ())), preferred_element_type=jnp.float32
    )


def contract_first(left, right):
    return lax.dot_general(
        left, right, (((0,), (0,)), ((), ())), preferred_element_type=jnp.float32
    )


def bucket_layout(lengths_row, slot_count):
    seq_ends = jnp.cumsum(lengths_row)
    slot_places = jnp.arange(slot_count, dtype=jnp.int32)
    ended_mask = seq_ends[None, :] <= slot_places[:, None]
    segment = jnp.sum(ended_mask.astype(jnp.int32), axis=1)
    before_total = jnp.sum(jnp.where(ended_mask, lengths_row[None, :], 0), axis=1)
    return (segment, slot_places - before_total, slot_places < seq_ends[-1])


def rope_tables(position, head_size):
    half_size = head_size // 2
    frequency = jnp.exp(
        jnp.arange(half_size, dtype=jnp.float32) * (-2.0 * math.log(10000.0) / head_size)
    )
    angles = position.astype(jnp.float32)[:, None] * frequency[None, :]
    return (jnp.cos(angles), jnp.sin(angles))


def rotate(matrix, cosine, sine, head_count):
    row_count = matrix.shape[0]
    halves = matrix.reshape(row_count, head_count, 2, -1)
    first_half = halves[:, :, 0]
    second_half = halves[:, :, 1]
    cos_table = cosine[:, None, :]
    sin_table = sine[:, None, :]
    turned = jnp.stack(
        [
            first_half * cos_table - second_half * sin_table,
            second_half * cos_table + first_half * sin_table,
        ],
        axis=2,
    )
    return turned.reshape(row_count, -1)


def allowed_mask(segment, valid):
    slot_places = jnp.arange(segment.shape[0])
    earlier = slot_places[None, :] < slot_places[:, None]
    same_seq = segment[:, None] == segment[None, :]
    diagonal = slot_places[None, :] == slot_places[:, None]
    return diagonal | same_seq & earlier & valid[:, None]


def rms_scale(matrix):
    return lax.rsqrt(jnp.mean(matrix * matrix, axis=-1, keepdims=True) + EPSILON)


def masked_scores(query_heads, key_heads, allowed, score_scale):
    raw_scores = (
        jnp.einsum("qhd,khd->hqk", query_heads, key_heads, preferred_element_type=jnp.float32)
        * score_scale
    )
    return jnp.where(allowed[None], raw_scores, -1e30)


AXES = ("dp", "fsdp")


def flip(value, bit, device_count):
    pairs = [(place, place ^ (1 << bit)) for place in range(device_count)]
    return lax.ppermute(value, AXES, pairs)


def stage_orders(dp_size, fsdp_size):
    bit_count = (dp_size * fsdp_size).bit_length() - 1
    core_bit = fsdp_size.bit_length() - 1
    high_bits = list(range(core_bit + 1, bit_count))
    rest = list(range(1, core_bit))
    return ([core_bit] + high_bits + [0] + rest, [core_bit, 0] + high_bits + rest)


def reduce_rows(partial_sum, order, place, device_count):
    bit_count = len(order)
    row_count, width = partial_sum.shape
    current = partial_sum.reshape((2,) * bit_count + (row_count // device_count, width))
    left = list(range(bit_count - 1, -1, -1))
    for step, bit in enumerate(order):
        axis = left.index(bit)
        mine = (place >> bit) & 1
        sent = lax.dynamic_index_in_dim(current, 1 - mine, axis, keepdims=False)
        kept = lax.dynamic_index_in_dim(current, mine, axis, keepdims=False)
        got = flip(sent.astype(jnp.bfloat16), bit, device_count)
        current = kept.astype(jnp.float32) + got.astype(jnp.float32)
        if step + 1 < bit_count:
            current = current.astype(jnp.bfloat16)
        left.remove(bit)
    return current


def shards(
    dp_size,
    fsdp_size,
    tokens,
    first_values,
    cotangent,
    lengths,
    w_query,
    w_key,
    w_value,
    w_out,
    w_gate,
    w_up,
    w_down,
    gain_one,
    gain_two,
):
    device_count = dp_size * fsdp_size
    place = lax.axis_index("dp") * fsdp_size + lax.axis_index("fsdp")
    order_a, order_b = stage_orders(dp_size, fsdp_size)
    micro_count = lengths.shape[0]
    token_count, model_width = tokens.shape
    slot_count = token_count // micro_count
    head_count = HEADS
    head_size = model_width // head_count
    hidden_width = w_gate.shape[1]
    group_heads = 4
    group_count = head_count // group_heads
    score_scale = head_size ** (-0.5)

    gains = jnp.pad(jnp.stack([gain_one, gain_two], axis=1), ((0, 0), (0, 126)))
    first_set = lax.all_gather(
        jnp.concatenate([w_query, w_key, w_value, gains], axis=1), AXES, axis=0, tiled=True
    )
    second_set = lax.all_gather(
        jnp.concatenate([w_out, w_gate, w_up], axis=1), AXES, axis=0, tiled=True
    )
    down_w = lax.all_gather(w_down, AXES, axis=0, tiled=True)
    query_w = first_set[:, :model_width]
    key_w = first_set[:, model_width : 2 * model_width]
    value_w = first_set[:, 2 * model_width : 3 * model_width]
    gain_first_f = first_set[:, 3 * model_width].astype(jnp.float32)[None, :]
    gain_second_f = first_set[:, 3 * model_width + 1].astype(jnp.float32)[None, :]
    out_w = second_set[:, :model_width]
    gate_w = second_set[:, model_width : model_width + hidden_width]
    up_w = second_set[:, model_width + hidden_width :]

    inputs = tokens.astype(jnp.float32)
    first_input = first_values.astype(jnp.float32)
    layouts = [bucket_layout(lengths[index], slot_count) for index in range(micro_count)]
    position = jnp.concatenate([layout[1] for layout in layouts])
    valid = jnp.concatenate([layout[2] for layout in layouts])
    cosine, sine = rope_tables(position, head_size)
    allowed = [allowed_mask(layout[0], layout[2]) for layout in layouts]
    scale_one = rms_scale(inputs)
    normed = (inputs * scale_one * gain_first_f).astype(jnp.bfloat16)
    query_rot = rotate(forward_dot(normed, query_w), cosine, sine, head_count).astype(jnp.bfloat16)
    key_rot = rotate(forward_dot(normed, key_w), cosine, sine, head_count).astype(jnp.bfloat16)
    value_mix = (0.5 * forward_dot(normed, value_w) + 0.5 * first_input).astype(jnp.bfloat16)
    shape = (micro_count, slot_count, head_count, head_size)
    query_heads = query_rot.reshape(shape)
    key_heads = key_rot.reshape(shape)
    value_heads = value_mix.reshape(shape)
    contexts = []
    log_masses = []
    for index in range(micro_count):
        context_parts = []
        for group_index in range(group_count):
            head_lo = group_index * group_heads
            head_hi = head_lo + group_heads
            scores = masked_scores(
                query_heads[index, :, head_lo:head_hi],
                key_heads[index, :, head_lo:head_hi],
                allowed[index],
                score_scale,
            )
            top_score = jnp.max(scores, axis=-1, keepdims=True)
            exp_scores = jnp.exp(scores - top_score)
            total_mass = jnp.sum(exp_scores, axis=-1, keepdims=True)
            prob_low = (exp_scores / total_mass).astype(jnp.bfloat16)
            log_masses.append(top_score + jnp.log(total_mass))
            context_parts.append(
                jnp.einsum(
                    "hqk,khd->qhd",
                    prob_low,
                    value_heads[index, :, head_lo:head_hi],
                    preferred_element_type=jnp.float32,
                )
            )
        contexts.append(jnp.concatenate(context_parts, axis=1).reshape(slot_count, model_width))
    context = jnp.concatenate(contexts, axis=0).astype(jnp.bfloat16)
    hidden = inputs + forward_dot(context, out_w)
    scale_two = rms_scale(hidden)
    normed_two = (hidden * scale_two * gain_second_f).astype(jnp.bfloat16)
    gate_values = forward_dot(normed_two, gate_w)
    upward = forward_dot(normed_two, up_w)
    sigmoid_gate = jax.nn.sigmoid(gate_values)
    silu_gate = gate_values * sigmoid_gate
    product = (silu_gate * upward).astype(jnp.bfloat16)
    out_tokens = (hidden + forward_dot(product, down_w)).astype(jnp.bfloat16)

    grad_y = cotangent.astype(jnp.float32) * valid.astype(jnp.float32)[:, None]
    grad_y_low = grad_y.astype(jnp.bfloat16)
    grad_down_w = contract_first(product, grad_y_low).astype(jnp.bfloat16)
    grad_down_sum = reduce_rows(grad_down_w, order_a, place, device_count)
    grad_product = contract_last(grad_y_low, down_w)
    grad_upward = (grad_product * silu_gate).astype(jnp.bfloat16)
    grad_gate_low = (
        grad_product * upward * sigmoid_gate * (1.0 + gate_values * (1.0 - sigmoid_gate))
    ).astype(jnp.bfloat16)
    grad_gate_w = contract_first(normed_two, grad_gate_low).astype(jnp.bfloat16)
    grad_gate_sum = reduce_rows(grad_gate_w, order_b, place, device_count)
    grad_up_w = contract_first(normed_two, grad_upward).astype(jnp.bfloat16)
    grad_up_sum = reduce_rows(grad_up_w, order_a, place, device_count)
    grad_normed_two = contract_last(grad_gate_low, gate_w) + contract_last(grad_upward, up_w)
    grad_gain_second = jnp.sum(grad_normed_two * hidden * scale_two, axis=0)
    inner_two = grad_normed_two * gain_second_f
    grad_hidden = (
        grad_y
        + scale_two * inner_two
        - hidden * scale_two**3 * jnp.mean(inner_two * hidden, axis=-1, keepdims=True)
    )
    grad_hidden_low = grad_hidden.astype(jnp.bfloat16)
    grad_out_w = contract_first(context, grad_hidden_low).astype(jnp.bfloat16)
    grad_out_sum = reduce_rows(grad_out_w, order_b, place, device_count)
    grad_context = contract_last(grad_hidden_low, out_w).astype(jnp.bfloat16)
    grad_context_heads = grad_context.reshape(shape)
    value_grads = []
    query_grads = []
    key_grads = []
    for index in range(micro_count):
        value_grad_parts = []
        query_grad_parts = []
        key_grad_parts = []
        for group_index in range(group_count):
            head_lo = group_index * group_heads
            head_hi = head_lo + group_heads
            query_part = query_heads[index, :, head_lo:head_hi]
            key_part = key_heads[index, :, head_lo:head_hi]
            value_part = value_heads[index, :, head_lo:head_hi]
            context_grad_part = grad_context_heads[index, :, head_lo:head_hi]
            scores_again = masked_scores(query_part, key_part, allowed[index], score_scale)
            prob_full = jnp.exp(scores_again - log_masses[index * group_count + group_index])
            prob_again = prob_full.astype(jnp.bfloat16)
            value_grad_parts.append(
                jnp.einsum(
                    "hqk,qhd->khd",
                    prob_again,
                    context_grad_part,
                    preferred_element_type=jnp.float32,
                )
            )
            grad_probs = jnp.einsum(
                "qhd,khd->hqk", context_grad_part, value_part, preferred_element_type=jnp.float32
            )
            grad_scores = prob_full * (
                grad_probs - jnp.sum(prob_full * grad_probs, axis=-1, keepdims=True)
            )
            grad_scores_low = grad_scores.astype(jnp.bfloat16)
            query_grad_parts.append(
                jnp.einsum(
                    "hqk,khd->qhd", grad_scores_low, key_part, preferred_element_type=jnp.float32
                )
                * score_scale
            )
            key_grad_parts.append(
                jnp.einsum(
                    "hqk,qhd->khd", grad_scores_low, query_part, preferred_element_type=jnp.float32
                )
                * score_scale
            )
        flat = (slot_count, model_width)
        value_grads.append(jnp.concatenate(value_grad_parts, axis=1).reshape(flat))
        query_grads.append(jnp.concatenate(query_grad_parts, axis=1).reshape(flat))
        key_grads.append(jnp.concatenate(key_grad_parts, axis=1).reshape(flat))
    grad_value_full = jnp.concatenate(value_grads, axis=0)
    grad_query_low = rotate(
        jnp.concatenate(query_grads, axis=0), cosine, -sine, head_count
    ).astype(jnp.bfloat16)
    grad_key_low = rotate(jnp.concatenate(key_grads, axis=0), cosine, -sine, head_count).astype(
        jnp.bfloat16
    )
    grad_first = 0.5 * grad_value_full
    grad_value_low = grad_first.astype(jnp.bfloat16)
    grad_query_w = contract_first(normed, grad_query_low).astype(jnp.bfloat16)
    grad_key_w = contract_first(normed, grad_key_low).astype(jnp.bfloat16)
    grad_value_w = contract_first(normed, grad_value_low).astype(jnp.bfloat16)
    grad_normed = (
        contract_last(grad_query_low, query_w)
        + contract_last(grad_key_low, key_w)
        + contract_last(grad_value_low, value_w)
    )
    grad_gain_first = jnp.sum(grad_normed * inputs * scale_one, axis=0)
    inner_one = grad_normed * gain_first_f
    grad_tokens = (
        grad_hidden
        + scale_one * inner_one
        - inputs * scale_one**3 * jnp.mean(inner_one * inputs, axis=-1, keepdims=True)
    )
    grad_query_sum = reduce_rows(grad_query_w, order_a, place, device_count)
    grad_key_sum = reduce_rows(grad_key_w, order_b, place, device_count)
    grad_value_sum = reduce_rows(grad_value_w, order_a, place, device_count)
    gain_columns = jnp.pad(
        jnp.stack([grad_gain_first, grad_gain_second], axis=1), ((0, 0), (0, 126))
    )
    grad_gains = reduce_rows(gain_columns, order_b, place, device_count)
    return (
        out_tokens,
        grad_tokens,
        grad_first,
        grad_query_sum,
        grad_key_sum,
        grad_value_sum,
        grad_out_sum,
        grad_gate_sum,
        grad_up_sum,
        grad_down_sum,
        grad_gains[:, 0],
        grad_gains[:, 1],
    )


def solution(mesh):
    rows = P(AXES, None)
    ends = P(AXES)
    return jax.shard_map(
        partial(shards, mesh.shape["dp"], mesh.shape["fsdp"]),
        mesh=mesh,
        in_specs=(rows,) * 11 + (ends,) * 2,
        out_specs=(rows,) * 10 + (ends,) * 2,
        check_vma=False,
    )
```

```python
import math
from functools import partial

import jax
import jax.numpy as jnp
from jax import lax
from jax.experimental import pallas as pl
from jax.experimental.pallas import tpu as pltpu
from jax.sharding import PartitionSpec as P

HEADS = 16


EPSILON = 1e-06


def forward_dot(left, right):
    return jnp.dot(left, right, preferred_element_type=jnp.float32)


def contract_last(left, right):
    return lax.dot_general(
        left, right, (((1,), (1,)), ((), ())), preferred_element_type=jnp.float32
    )


def contract_first(left, right):
    return lax.dot_general(
        left, right, (((0,), (0,)), ((), ())), preferred_element_type=jnp.float32
    )


def bucket_layout(lengths_row, slot_count):
    seq_ends = jnp.cumsum(lengths_row)
    slot_places = jnp.arange(slot_count, dtype=jnp.int32)
    ended_mask = seq_ends[None, :] <= slot_places[:, None]
    segment = jnp.sum(ended_mask.astype(jnp.int32), axis=1)
    before_total = jnp.sum(jnp.where(ended_mask, lengths_row[None, :], 0), axis=1)
    return (segment, slot_places - before_total, slot_places < seq_ends[-1])


def rope_tables(position, head_size):
    half_size = head_size // 2
    frequency = jnp.exp(
        jnp.arange(half_size, dtype=jnp.float32) * (-2.0 * math.log(10000.0) / head_size)
    )
    angles = position.astype(jnp.float32)[:, None] * frequency[None, :]
    return (jnp.cos(angles), jnp.sin(angles))


def allowed_mask(segment, valid):
    slot_places = jnp.arange(segment.shape[0])
    earlier = slot_places[None, :] < slot_places[:, None]
    same_seq = segment[:, None] == segment[None, :]
    diagonal = slot_places[None, :] == slot_places[:, None]
    return diagonal | same_seq & earlier & valid[:, None]


def rms_scale(matrix):
    return lax.rsqrt(jnp.mean(matrix * matrix, axis=-1, keepdims=True) + EPSILON)


PAIR = 128


def swap_halves(matrix, half_size):
    lane = lax.broadcasted_iota(jnp.int32, matrix.shape, 1)
    first = lane % (2 * half_size) < half_size
    width = matrix.shape[1]
    return jnp.where(
        first, pltpu.roll(matrix, width - half_size, 1), pltpu.roll(matrix, half_size, 1)
    )


def head_part(matrix, head, head_size):
    lane = lax.broadcasted_iota(jnp.int32, matrix.shape, 1)
    return jnp.where(lane // head_size == head, matrix, jnp.zeros_like(matrix))


def attend_kernel(
    slot_count,
    head_size,
    x_ref,
    scale_ref,
    gain_ref,
    wq_ref,
    wk_ref,
    wv_ref,
    first_ref,
    bias_ref,
    cos_ref,
    sin_ref,
    normed_ref,
    q_ref,
    k_ref,
    v_ref,
    ctx_ref,
    lse_ref,
):
    half_size = head_size // 2
    score_scale = head_size ** (-0.5)
    width = q_ref.shape[1]
    bucket_count = bias_ref.shape[0]
    query_rows = slot_count // 2

    @pl.when(pl.program_id(0) == 0)
    def _():
        normed_ref[...] = (
            x_ref[...].astype(jnp.float32) * scale_ref[...] * gain_ref[...]
        ).astype(jnp.bfloat16)

    normed = normed_ref[...]
    cosine = cos_ref[...]
    sine = sin_ref[...]
    for raw_ref, w_ref in ((q_ref, wq_ref), (k_ref, wk_ref)):
        raw = forward_dot(normed, w_ref[...])
        for low in range(0, width, PAIR):
            part = raw[:, low : low + PAIR]
            raw_ref[:, low : low + PAIR] = (
                part * cosine + swap_halves(part, half_size) * sine
            ).astype(jnp.bfloat16)
    v_ref[...] = (
        0.5 * forward_dot(normed, wv_ref[...]) + 0.5 * first_ref[...].astype(jnp.float32)
    ).astype(jnp.bfloat16)
    for bucket in range(bucket_count):
        base = bucket * slot_count
        for low in range(0, width, PAIR):
            keys = k_ref[base : base + slot_count, low : low + PAIR]
            queries = q_ref[base : base + slot_count, low : low + PAIR] * score_scale
            values_t = v_ref[base : base + slot_count, low : low + PAIR].T
            for start in range(0, slot_count, query_rows):
                end = start + query_rows
                parts = []
                for head in range(PAIR // head_size):
                    key_head = head_part(keys[:end], head, head_size)
                    scores = (
                        contract_last(key_head, queries[start:end])
                        + bias_ref[bucket, :end, start:end]
                    )
                    top = jnp.max(scores, axis=0, keepdims=True)
                    weights = jnp.exp(scores - top)
                    mass = jnp.sum(weights, axis=0, keepdims=True)
                    row = (low // head_size) + head
                    lse_ref[bucket, 0, row : row + 1, start:end] = top + jnp.log(mass)
                    mixed = forward_dot(
                        values_t[head * head_size : (head + 1) * head_size, :end],
                        weights.astype(jnp.bfloat16),
                    )
                    parts.append(mixed * (1.0 / mass))
                ctx_ref[base + start : base + end, low : low + PAIR] = (
                    jnp.concatenate(parts, axis=0).T.astype(jnp.bfloat16)
                )


def attend(inputs, scale_one, gain, weights, first_values, bias, cosine, sine, head_size, width):
    token_count, model_width = inputs.shape
    bucket_count, slot_count = bias.shape[:2]
    steps = model_width // width
    whole = lambda step: (0, 0)
    block = pl.BlockSpec((token_count, width), lambda step: (0, step))
    heads = width // head_size
    table = pl.BlockSpec((token_count, PAIR), whole)
    low_shape = jax.ShapeDtypeStruct((token_count, model_width), jnp.bfloat16)
    return pl.pallas_call(
        partial(attend_kernel, slot_count, head_size),
        grid=(steps,),
        in_specs=[
            pl.BlockSpec((token_count, model_width), whole),
            pl.BlockSpec((token_count, 1), whole),
            pl.BlockSpec((1, model_width), whole),
            pl.BlockSpec((model_width, width), lambda step: (0, step)),
            pl.BlockSpec((model_width, width), lambda step: (0, steps + step)),
            pl.BlockSpec((model_width, width), lambda step: (0, 2 * steps + step)),
            block,
            pl.BlockSpec((bucket_count, slot_count, slot_count), lambda step: (0, 0, 0)),
            table,
            table,
        ],
        out_specs=[
            pl.BlockSpec((token_count, model_width), whole),
            block,
            block,
            block,
            block,
            pl.BlockSpec((bucket_count, 1, heads, slot_count), lambda step: (0, step, 0, 0)),
        ],
        out_shape=[low_shape] * 5
        + [jax.ShapeDtypeStruct((bucket_count, steps, heads, slot_count), jnp.float32)],
        compiler_params=pltpu.CompilerParams(vmem_limit_bytes=56 << 20),
        name="attend",
    )(inputs, scale_one, gain, weights, weights, weights, first_values, bias, cosine, sine)


def attend_back_kernel(
    slot_count,
    head_size,
    q_ref,
    k_ref,
    v_ref,
    grad_ref,
    lse_ref,
    bias_ref,
    cos_ref,
    sin_ref,
    grads_ref,
    first_ref,
    dk_ref,
    dv_ref,
):
    half_size = head_size // 2
    score_scale = head_size ** (-0.5)
    width = q_ref.shape[1]
    bucket_count = bias_ref.shape[0]
    query_rows = slot_count // 2
    head_count = PAIR // head_size
    for bucket in range(bucket_count):
        base = bucket * slot_count
        cosine = cos_ref[base : base + slot_count]
        sine = sin_ref[base : base + slot_count]
        for low in range(0, width, PAIR):
            keys = k_ref[base : base + slot_count, low : low + PAIR]
            values = v_ref[base : base + slot_count, low : low + PAIR]
            queries = q_ref[base : base + slot_count, low : low + PAIR] * score_scale
            grads = grad_ref[base : base + slot_count, low : low + PAIR]
            keys_t = keys.T
            query_parts = []
            for start in range(0, slot_count, query_rows):
                end = start + query_rows
                parts = []
                for head in range(head_count):
                    row = (low // head_size) + head
                    scores = contract_last(
                        head_part(keys[:end], head, head_size), queries[start:end]
                    )
                    probs = jnp.exp(
                        scores
                        + bias_ref[bucket, :end, start:end]
                        - lse_ref[bucket, 0, row : row + 1, start:end]
                    )
                    grad_probs = contract_last(
                        head_part(values[:end], head, head_size), grads[start:end]
                    )
                    weighted = probs * grad_probs
                    grad_scores = (
                        weighted - probs * jnp.sum(weighted, axis=0, keepdims=True)
                    ).astype(jnp.bfloat16)
                    dv = forward_dot(probs.astype(jnp.bfloat16), grads[start:end])
                    dk = forward_dot(grad_scores, queries[start:end])
                    if start == 0:
                        dv_ref[head, :end] = dv
                        dk_ref[head, :end] = dk
                    else:
                        dv_ref[head, :start] += dv[:start]
                        dk_ref[head, :start] += dk[:start]
                        dv_ref[head, start:end] = dv[start:]
                        dk_ref[head, start:end] = dk[start:]
                    parts.append(
                        forward_dot(
                            keys_t[head * head_size : (head + 1) * head_size, :end], grad_scores
                        )
                    )
                query_parts.append((jnp.concatenate(parts, axis=0) * score_scale).T)
            lane = lax.broadcasted_iota(jnp.int32, (slot_count, PAIR), 1)
            dv = dv_ref[0]
            dk = dk_ref[0]
            for head in range(1, head_count):
                here = lane // head_size == head
                dv = jnp.where(here, dv_ref[head], dv)
                dk = jnp.where(here, dk_ref[head], dk)
            dq = jnp.concatenate(query_parts, axis=0)
            rows = slice(base, base + slot_count)
            for index, part in enumerate((dq, dk)):
                grads_ref[index, rows, low : low + PAIR] = (
                    part * cosine - swap_halves(part, half_size) * sine
                ).astype(jnp.bfloat16)
            first_ref[rows, low : low + PAIR] = 0.5 * dv
            grads_ref[2, rows, low : low + PAIR] = (0.5 * dv).astype(jnp.bfloat16)


def attend_back(
    queries, keys, values, grads, lse, bias, cosine, sine, head_size, width, first_step, steps
):
    token_count = queries.shape[0]
    bucket_count, slot_count = bias.shape[:2]
    heads = width // head_size
    block = pl.BlockSpec((token_count, width), lambda step: (0, first_step + step))
    table = pl.BlockSpec((token_count, PAIR), lambda step: (0, 0))
    return pl.pallas_call(
        partial(attend_back_kernel, slot_count, head_size),
        grid=(steps,),
        in_specs=[
            block,
            block,
            block,
            block,
            pl.BlockSpec(
                (bucket_count, 1, heads, slot_count), lambda step: (0, first_step + step, 0, 0)
            ),
            pl.BlockSpec((bucket_count, slot_count, slot_count), lambda step: (0, 0, 0)),
            table,
            table,
        ],
        out_specs=[
            pl.BlockSpec((3, token_count, width), lambda step: (0, 0, step)),
            pl.BlockSpec((token_count, width), lambda step: (0, step)),
        ],
        out_shape=[
            jax.ShapeDtypeStruct((3, token_count, steps * width), jnp.bfloat16),
            jax.ShapeDtypeStruct((token_count, steps * width), jnp.float32),
        ],
        scratch_shapes=[
            pltpu.VMEM((PAIR // head_size, slot_count, PAIR), jnp.float32),
            pltpu.VMEM((PAIR // head_size, slot_count, PAIR), jnp.float32),
        ],
        compiler_params=pltpu.CompilerParams(vmem_limit_bytes=56 << 20),
        name="attend_back",
    )(queries, keys, values, grads, lse, bias, cosine, sine)


AXES = ("dp", "fsdp")


def flip(value, bit, device_count):
    pairs = [(place, place ^ (1 << bit)) for place in range(device_count)]
    return lax.ppermute(value, AXES, pairs)


def stage_orders(dp_size, fsdp_size):
    bit_count = (dp_size * fsdp_size).bit_length() - 1
    core_bit = fsdp_size.bit_length() - 1
    high_bits = list(range(core_bit + 1, bit_count))
    rest = list(range(1, core_bit))
    return ([core_bit] + high_bits + [0] + rest, [core_bit, 0] + high_bits + rest)


def reduce_rows(partial_sum, order, place, device_count):
    bit_count = len(order)
    row_count, width = partial_sum.shape
    current = partial_sum.reshape((2,) * bit_count + (row_count // device_count, width))
    left = list(range(bit_count - 1, -1, -1))
    for step, bit in enumerate(order):
        axis = left.index(bit)
        mine = (place >> bit) & 1
        sent = lax.dynamic_index_in_dim(current, 1 - mine, axis, keepdims=False)
        kept = lax.dynamic_index_in_dim(current, mine, axis, keepdims=False)
        got = flip(sent.astype(jnp.bfloat16), bit, device_count)
        current = kept.astype(jnp.float32) + got.astype(jnp.float32)
        if step + 1 < bit_count:
            current = current.astype(jnp.bfloat16)
        left.remove(bit)
    return current


def shards(
    dp_size,
    fsdp_size,
    tokens,
    first_values,
    cotangent,
    lengths,
    w_query,
    w_key,
    w_value,
    w_out,
    w_gate,
    w_up,
    w_down,
    gain_one,
    gain_two,
):
    device_count = dp_size * fsdp_size
    place = lax.axis_index("dp") * fsdp_size + lax.axis_index("fsdp")
    order_a, order_b = stage_orders(dp_size, fsdp_size)
    micro_count = lengths.shape[0]
    token_count, model_width = tokens.shape
    slot_count = token_count // micro_count
    head_count = HEADS
    head_size = model_width // head_count
    hidden_width = w_gate.shape[1]

    gains = jnp.pad(jnp.stack([gain_one, gain_two], axis=1), ((0, 0), (0, 126)))
    first_set = lax.all_gather(
        jnp.concatenate([w_query, w_key, w_value, gains], axis=1), AXES, axis=0, tiled=True
    )
    second_set = lax.all_gather(
        jnp.concatenate([w_out, w_gate, w_up], axis=1), AXES, axis=0, tiled=True
    )
    down_w = lax.all_gather(w_down, AXES, axis=0, tiled=True)
    query_w = first_set[:, :model_width]
    key_w = first_set[:, model_width : 2 * model_width]
    value_w = first_set[:, 2 * model_width : 3 * model_width]
    gain_first_f = first_set[:, 3 * model_width].astype(jnp.float32)[None, :]
    gain_second_f = first_set[:, 3 * model_width + 1].astype(jnp.float32)[None, :]
    out_w = second_set[:, :model_width]
    gate_w = second_set[:, model_width : model_width + hidden_width]
    up_w = second_set[:, model_width + hidden_width :]

    inputs = tokens.astype(jnp.float32)
    layouts = [bucket_layout(lengths[index], slot_count) for index in range(micro_count)]
    position = jnp.concatenate([layout[1] for layout in layouts])
    valid = jnp.concatenate([layout[2] for layout in layouts])
    cosine, sine = rope_tables(position, head_size)
    cosine = jnp.tile(cosine, (1, 2 * PAIR // head_size))
    sine = jnp.tile(jnp.concatenate([-sine, sine], axis=1), (1, PAIR // head_size))
    bias = jnp.stack(
        [
            jnp.where(allowed_mask(layout[0], layout[2]).T, 0.0, -1e30).astype(jnp.float32)
            for layout in layouts
        ]
    )
    scale_one = rms_scale(inputs)
    width = 4 * head_size
    normed, query_rot, key_rot, value_mix, context, lse = attend(
        tokens,
        scale_one,
        gain_first_f,
        first_set,
        first_values,
        bias,
        cosine,
        sine,
        head_size,
        width,
    )
    hidden = inputs + forward_dot(context, out_w)
    scale_two = rms_scale(hidden)
    normed_two = (hidden * scale_two * gain_second_f).astype(jnp.bfloat16)
    gate_values = forward_dot(normed_two, gate_w)
    upward = forward_dot(normed_two, up_w)
    sigmoid_gate = jax.nn.sigmoid(gate_values)
    silu_gate = gate_values * sigmoid_gate
    product = (silu_gate * upward).astype(jnp.bfloat16)
    out_tokens = (hidden + forward_dot(product, down_w)).astype(jnp.bfloat16)

    grad_y = cotangent.astype(jnp.float32) * valid.astype(jnp.float32)[:, None]
    grad_y_low = grad_y.astype(jnp.bfloat16)
    grad_down_w = contract_first(product, grad_y_low).astype(jnp.bfloat16)
    grad_down_sum = reduce_rows(grad_down_w, order_a, place, device_count)
    grad_product = contract_last(grad_y_low, down_w)
    grad_upward = (grad_product * silu_gate).astype(jnp.bfloat16)
    grad_gate_low = (
        grad_product * upward * sigmoid_gate * (1.0 + gate_values * (1.0 - sigmoid_gate))
    ).astype(jnp.bfloat16)
    grad_gate_w = contract_first(normed_two, grad_gate_low).astype(jnp.bfloat16)
    grad_gate_sum = reduce_rows(grad_gate_w, order_b, place, device_count)
    grad_up_w = contract_first(normed_two, grad_upward).astype(jnp.bfloat16)
    grad_up_sum = reduce_rows(grad_up_w, order_a, place, device_count)
    grad_normed_two = contract_last(grad_gate_low, gate_w) + contract_last(grad_upward, up_w)
    grad_gain_second = jnp.sum(grad_normed_two * hidden * scale_two, axis=0)
    inner_two = grad_normed_two * gain_second_f
    grad_hidden = (
        grad_y
        + scale_two * inner_two
        - hidden * scale_two**3 * jnp.mean(inner_two * hidden, axis=-1, keepdims=True)
    )
    grad_hidden_low = grad_hidden.astype(jnp.bfloat16)
    grad_out_w = contract_first(context, grad_hidden_low).astype(jnp.bfloat16)
    grad_out_sum = reduce_rows(grad_out_w, order_b, place, device_count)
    grad_context = contract_last(grad_hidden_low, out_w).astype(jnp.bfloat16)
    steps = model_width // width
    half_steps = steps // 2
    halves = [
        attend_back(
            query_rot,
            key_rot,
            value_mix,
            grad_context,
            lse,
            bias,
            cosine,
            sine,
            head_size,
            width,
            half * half_steps,
            half_steps,
        )
        for half in range(2)
    ]
    grad_first = jnp.concatenate([half[1] for half in halves], axis=1)
    grad_query_low, grad_key_low, grad_value_low = [
        jnp.concatenate([half[0][index] for half in halves], axis=1) for index in range(3)
    ]
    grad_query_w = contract_first(normed, grad_query_low).astype(jnp.bfloat16)
    grad_key_w = contract_first(normed, grad_key_low).astype(jnp.bfloat16)
    grad_value_w = contract_first(normed, grad_value_low).astype(jnp.bfloat16)
    grad_normed = (
        contract_last(grad_query_low, query_w)
        + contract_last(grad_key_low, key_w)
        + contract_last(grad_value_low, value_w)
    )
    grad_gain_first = jnp.sum(grad_normed * inputs * scale_one, axis=0)
    inner_one = grad_normed * gain_first_f
    grad_tokens = (
        grad_hidden
        + scale_one * inner_one
        - inputs * scale_one**3 * jnp.mean(inner_one * inputs, axis=-1, keepdims=True)
    )
    grad_query_sum = reduce_rows(grad_query_w, order_a, place, device_count)
    grad_key_sum = reduce_rows(grad_key_w, order_b, place, device_count)
    grad_value_sum = reduce_rows(grad_value_w, order_a, place, device_count)
    gain_columns = jnp.pad(
        jnp.stack([grad_gain_first, grad_gain_second], axis=1), ((0, 0), (0, 126))
    )
    grad_gains = reduce_rows(gain_columns, order_b, place, device_count)
    return (
        out_tokens,
        grad_tokens,
        grad_first,
        grad_query_sum,
        grad_key_sum,
        grad_value_sum,
        grad_out_sum,
        grad_gate_sum,
        grad_up_sum,
        grad_down_sum,
        grad_gains[:, 0],
        grad_gains[:, 1],
    )


def solution(mesh):
    rows = P(AXES, None)
    ends = P(AXES)
    return jax.shard_map(
        partial(shards, mesh.shape["dp"], mesh.shape["fsdp"]),
        mesh=mesh,
        in_specs=(rows,) * 11 + (ends,) * 2,
        out_specs=(rows,) * 10 + (ends,) * 2,
        check_vma=False,
    )
```

```python
import math
from functools import partial

import jax
import jax.numpy as jnp
from jax import lax
from jax.experimental import pallas as pl
from jax.experimental.pallas import tpu as pltpu
from jax.sharding import PartitionSpec as P

HEADS = 16


EPSILON = 1e-06


def forward_dot(left, right):
    return jnp.dot(left, right, preferred_element_type=jnp.float32)


def contract_last(left, right):
    return lax.dot_general(
        left, right, (((1,), (1,)), ((), ())), preferred_element_type=jnp.float32
    )


def contract_first(left, right):
    return lax.dot_general(
        left, right, (((0,), (0,)), ((), ())), preferred_element_type=jnp.float32
    )


def bucket_layout(lengths_row, slot_count):
    seq_ends = jnp.cumsum(lengths_row)
    slot_places = jnp.arange(slot_count, dtype=jnp.int32)
    ended_mask = seq_ends[None, :] <= slot_places[:, None]
    segment = jnp.sum(ended_mask.astype(jnp.int32), axis=1)
    before_total = jnp.sum(jnp.where(ended_mask, lengths_row[None, :], 0), axis=1)
    return (segment, slot_places - before_total, slot_places < seq_ends[-1])


def rope_tables(position, head_size):
    half_size = head_size // 2
    frequency = jnp.exp(
        jnp.arange(half_size, dtype=jnp.float32) * (-2.0 * math.log(10000.0) / head_size)
    )
    angles = position.astype(jnp.float32)[:, None] * frequency[None, :]
    return (jnp.cos(angles), jnp.sin(angles))


def allowed_mask(segment, valid):
    slot_places = jnp.arange(segment.shape[0])
    earlier = slot_places[None, :] < slot_places[:, None]
    same_seq = segment[:, None] == segment[None, :]
    diagonal = slot_places[None, :] == slot_places[:, None]
    return diagonal | same_seq & earlier & valid[:, None]


def rms_scale(matrix):
    return lax.rsqrt(jnp.mean(matrix * matrix, axis=-1, keepdims=True) + EPSILON)


PAIR = 128


def swap_halves(matrix, half_size):
    lane = lax.broadcasted_iota(jnp.int32, matrix.shape, 1)
    first = lane % (2 * half_size) < half_size
    width = matrix.shape[1]
    return jnp.where(
        first, pltpu.roll(matrix, width - half_size, 1), pltpu.roll(matrix, half_size, 1)
    )


def head_part(matrix, head, head_size):
    lane = lax.broadcasted_iota(jnp.int32, matrix.shape, 1)
    return jnp.where(lane // head_size == head, matrix, jnp.zeros_like(matrix))


def attend_kernel(
    slot_count,
    head_size,
    normed_ref,
    wq_ref,
    wk_ref,
    wv_ref,
    first_ref,
    bias_ref,
    cos_ref,
    sin_ref,
    q_ref,
    k_ref,
    v_ref,
    ctx_ref,
    lse_ref,
):
    half_size = head_size // 2
    score_scale = head_size ** (-0.5)
    width = q_ref.shape[1]
    bucket_count = bias_ref.shape[0]
    query_rows = slot_count // 2
    normed = normed_ref[...]
    cosine = cos_ref[...]
    sine = sin_ref[...]
    for raw_ref, w_ref in ((q_ref, wq_ref), (k_ref, wk_ref)):
        raw = forward_dot(normed, w_ref[...])
        for low in range(0, width, PAIR):
            part = raw[:, low : low + PAIR]
            raw_ref[:, low : low + PAIR] = (
                part * cosine + swap_halves(part, half_size) * sine
            ).astype(jnp.bfloat16)
    v_ref[...] = (
        0.5 * forward_dot(normed, wv_ref[...]) + 0.5 * first_ref[...].astype(jnp.float32)
    ).astype(jnp.bfloat16)
    for bucket in range(bucket_count):
        base = bucket * slot_count
        for low in range(0, width, PAIR):
            keys = k_ref[base : base + slot_count, low : low + PAIR]
            queries = q_ref[base : base + slot_count, low : low + PAIR] * score_scale
            values_t = v_ref[base : base + slot_count, low : low + PAIR].T
            for start in range(0, slot_count, query_rows):
                end = start + query_rows
                parts = []
                for head in range(PAIR // head_size):
                    key_head = head_part(keys[:end], head, head_size)
                    scores = (
                        contract_last(key_head, queries[start:end])
                        + bias_ref[bucket, :end, start:end]
                    )
                    top = jnp.max(scores, axis=0, keepdims=True)
                    weights = jnp.exp(scores - top)
                    mass = jnp.sum(weights, axis=0, keepdims=True)
                    row = (low // head_size) + head
                    lse_ref[bucket, 0, row : row + 1, start:end] = top + jnp.log(mass)
                    mixed = forward_dot(
                        values_t[head * head_size : (head + 1) * head_size, :end],
                        weights.astype(jnp.bfloat16),
                    )
                    parts.append(mixed * (1.0 / mass))
                ctx_ref[base + start : base + end, low : low + PAIR] = (
                    jnp.concatenate(parts, axis=0).T.astype(jnp.bfloat16)
                )


def attend(normed, weights, first_values, bias, cosine, sine, head_size, width):
    token_count, model_width = normed.shape
    bucket_count, slot_count = bias.shape[:2]
    steps = model_width // width
    whole = lambda step: (0, 0)
    block = pl.BlockSpec((token_count, width), lambda step: (0, step))
    heads = width // head_size
    table = pl.BlockSpec((token_count, PAIR), whole)
    low_shape = jax.ShapeDtypeStruct((token_count, steps * width), jnp.bfloat16)
    return pl.pallas_call(
        partial(attend_kernel, slot_count, head_size),
        grid=(steps,),
        in_specs=[
            pl.BlockSpec((token_count, model_width), whole),
            pl.BlockSpec((model_width, width), lambda step: (0, step)),
            pl.BlockSpec((model_width, width), lambda step: (0, steps + step)),
            pl.BlockSpec((model_width, width), lambda step: (0, 2 * steps + step)),
            block,
            pl.BlockSpec((bucket_count, slot_count, slot_count), lambda step: (0, 0, 0)),
            table,
            table,
        ],
        out_specs=[
            block,
            block,
            block,
            block,
            pl.BlockSpec((bucket_count, 1, heads, slot_count), lambda step: (0, step, 0, 0)),
        ],
        out_shape=[low_shape] * 4
        + [jax.ShapeDtypeStruct((bucket_count, steps, heads, slot_count), jnp.float32)],
        compiler_params=pltpu.CompilerParams(vmem_limit_bytes=56 << 20),
        name="attend",
    )(normed, weights, weights, weights, first_values, bias, cosine, sine)


def attend_back_kernel(
    slot_count,
    head_size,
    q_ref,
    k_ref,
    v_ref,
    grad_ref,
    lse_ref,
    bias_ref,
    cos_ref,
    sin_ref,
    *rest,
):
    grads_ref, first_ref, dk_ref, dv_ref = rest[-4:]
    half_size = head_size // 2
    score_scale = head_size ** (-0.5)
    width = q_ref.shape[1]
    bucket_count = bias_ref.shape[0]
    query_rows = slot_count // 2
    head_count = PAIR // head_size
    for bucket in range(bucket_count):
        base = bucket * slot_count
        cosine = cos_ref[base : base + slot_count]
        sine = sin_ref[base : base + slot_count]
        for low in range(0, width, PAIR):
            keys = k_ref[base : base + slot_count, low : low + PAIR]
            values = v_ref[base : base + slot_count, low : low + PAIR]
            queries = q_ref[base : base + slot_count, low : low + PAIR] * score_scale
            grads = grad_ref[base : base + slot_count, low : low + PAIR]
            keys_t = keys.T
            query_parts = []
            for start in range(0, slot_count, query_rows):
                end = start + query_rows
                parts = []
                for head in range(head_count):
                    row = (low // head_size) + head
                    scores = contract_last(
                        head_part(keys[:end], head, head_size), queries[start:end]
                    )
                    probs = jnp.exp(
                        scores
                        + bias_ref[bucket, :end, start:end]
                        - lse_ref[bucket, 0, row : row + 1, start:end]
                    )
                    grad_probs = contract_last(
                        head_part(values[:end], head, head_size), grads[start:end]
                    )
                    weighted = probs * grad_probs
                    grad_scores = (
                        weighted - probs * jnp.sum(weighted, axis=0, keepdims=True)
                    ).astype(jnp.bfloat16)
                    dv = forward_dot(probs.astype(jnp.bfloat16), grads[start:end])
                    dk = forward_dot(grad_scores, queries[start:end])
                    if start == 0:
                        dv_ref[head, :end] = dv
                        dk_ref[head, :end] = dk
                    else:
                        dv_ref[head, :start] += dv[:start]
                        dk_ref[head, :start] += dk[:start]
                        dv_ref[head, start:end] = dv[start:]
                        dk_ref[head, start:end] = dk[start:]
                    parts.append(
                        forward_dot(
                            keys_t[head * head_size : (head + 1) * head_size, :end], grad_scores
                        )
                    )
                query_parts.append((jnp.concatenate(parts, axis=0) * score_scale).T)
            lane = lax.broadcasted_iota(jnp.int32, (slot_count, PAIR), 1)
            dv = dv_ref[0]
            dk = dk_ref[0]
            for head in range(1, head_count):
                here = lane // head_size == head
                dv = jnp.where(here, dv_ref[head], dv)
                dk = jnp.where(here, dk_ref[head], dk)
            dq = jnp.concatenate(query_parts, axis=0)
            rows = slice(base, base + slot_count)
            for index, part in enumerate((dq, dk)):
                grads_ref[index, rows, low : low + PAIR] = (
                    part * cosine - swap_halves(part, half_size) * sine
                ).astype(jnp.bfloat16)
            first_ref[rows, low : low + PAIR] = 0.5 * dv
            grads_ref[2, rows, low : low + PAIR] = (0.5 * dv).astype(jnp.bfloat16)


def attend_back(
    queries, keys, values, grads, lse, bias, cosine, sine, head_size, width, first_step, steps, first
):
    token_count, model_width = queries.shape
    bucket_count, slot_count = bias.shape[:2]
    heads = width // head_size
    block = pl.BlockSpec((token_count, width), lambda step: (0, first_step + step))
    table = pl.BlockSpec((token_count, PAIR), lambda step: (0, 0))
    shared = [] if first is None else [first]
    return pl.pallas_call(
        partial(attend_back_kernel, slot_count, head_size),
        grid=(steps,),
        in_specs=[
            block,
            block,
            block,
            block,
            pl.BlockSpec(
                (bucket_count, 1, heads, slot_count), lambda step: (0, first_step + step, 0, 0)
            ),
            pl.BlockSpec((bucket_count, slot_count, slot_count), lambda step: (0, 0, 0)),
            table,
            table,
        ]
        + [pl.BlockSpec(memory_space=pl.ANY)] * len(shared),
        out_specs=[
            pl.BlockSpec((3, token_count, width), lambda step: (0, 0, step)),
            block,
        ],
        out_shape=[
            jax.ShapeDtypeStruct((3, token_count, steps * width), jnp.bfloat16),
            jax.ShapeDtypeStruct((token_count, model_width), jnp.float32),
        ],
        scratch_shapes=[
            pltpu.VMEM((PAIR // head_size, slot_count, PAIR), jnp.float32),
            pltpu.VMEM((PAIR // head_size, slot_count, PAIR), jnp.float32),
        ],
        input_output_aliases={8: 1} if shared else {},
        compiler_params=pltpu.CompilerParams(vmem_limit_bytes=56 << 20),
        name="attend_back",
    )(queries, keys, values, grads, lse, bias, cosine, sine, *shared)


AXES = ("dp", "fsdp")


def flip(value, mask, device_count):
    pairs = [(place, place ^ mask) for place in range(device_count)]
    return lax.ppermute(value, AXES, pairs)


def masks_of(bits):
    masks = [0]
    for bit in bits:
        masks += [mask | 1 << bit for mask in masks]
    return masks


class Exchange:
    def __init__(self, partial_sum, steps, place, device_count):
        self.current = partial_sum
        self.steps = [list(step) for step in steps]
        self.left = sorted([bit for step in steps for bit in step], reverse=True)
        self.place = place
        self.device_count = device_count
        self.got = None

    def part(self, mask):
        value = self.current
        left = list(self.left)
        for bit in self.steps[0]:
            lead, row_count, width = value.shape
            high = 1 << left.index(bit)
            view = value.reshape(lead, high, 2, row_count // (2 * high), width)
            chosen = ((self.place ^ mask) >> bit) & 1
            value = lax.dynamic_index_in_dim(view, chosen, 2, keepdims=False)
            value = value.reshape(lead, row_count // 2, width)
            left.remove(bit)
        return value

    def outgoing(self):
        masks = masks_of(self.steps[0])
        self.kept = self.part(0)
        return [self.part(mask) for mask in masks[1:]]

    def launch(self, sent):
        masks = masks_of(self.steps[0])[1:]
        self.got = [flip(value, mask, self.device_count) for value, mask in zip(sent, masks)]

    def settle(self, got):
        total = self.kept.astype(jnp.float32)
        for value in got:
            total = total + value.astype(jnp.float32)
        for bit in self.steps.pop(0):
            self.left.remove(bit)
        self.current = total.astype(jnp.bfloat16) if self.steps else total


class Gather:
    def __init__(self, rows, steps, place, device_count):
        self.current = rows
        self.steps = [list(step) for step in steps]
        self.have = []
        self.place = place
        self.device_count = device_count
        self.got = None

    def outgoing(self):
        return [self.current]

    def launch(self, sent):
        masks = masks_of(self.steps[0])[1:]
        self.got = [flip(sent[0], mask, self.device_count) for mask in masks]

    def settle(self, got):
        pieces = [self.current] + list(got)
        for bit in self.steps.pop(0):
            row_count, width = pieces[0].shape
            high = 1 << len([other for other in self.have if other > bit])
            shape = (high, 1, row_count // high, width)
            side = lax.broadcasted_iota(jnp.int32, (1, 2, 1, 1), 1)
            mine = side == ((self.place >> bit) & 1)
            pieces = [
                jnp.where(mine, near.reshape(shape), far.reshape(shape)).reshape(
                    2 * row_count, width
                )
                for near, far in zip(pieces[0::2], pieces[1::2])
            ]
            self.have.append(bit)
        self.current = pieces[0]


def tick(chain, settled, launched):
    settled = [item for item in settled if item.got is not None]
    if settled:
        chain, gots = lax.optimization_barrier((chain, [item.got for item in settled]))
        for item, got in zip(settled, gots):
            item.settle(got)
            item.got = None
    launched = [item for item in launched if item.steps and item.got is None]
    if launched:
        chain, sents = lax.optimization_barrier((chain, [item.outgoing() for item in launched]))
        for item, sent in zip(launched, sents):
            item.launch(sent)
    return chain


def step_plans(dp_size, fsdp_size):
    bit_count = (dp_size * fsdp_size).bit_length() - 1
    core_bit = fsdp_size.bit_length() - 1
    high = list(range(core_bit + 1, bit_count))
    rest = list(range(1, core_bit))
    pairs = [rest[index : index + 2] for index in range(0, len(rest), 2)]
    core = [core_bit]
    return {
        "high_first": [core, high, [0]] + pairs,
        "low_first": [core, [0], high] + pairs,
        "short": [core, high + [0]] + pairs,
        "gather": pairs[::-1] + [[0] + high, core],
        "gather_low_first": pairs[::-1] + [[0], high, core],
        "gather_high_first": pairs[::-1] + [high, [0], core],
    }


def shards(
    dp_size,
    fsdp_size,
    tokens,
    first_values,
    cotangent,
    lengths,
    w_query,
    w_key,
    w_value,
    w_out,
    w_gate,
    w_up,
    w_down,
    gain_one,
    gain_two,
):
    device_count = dp_size * fsdp_size
    place = lax.axis_index("dp") * fsdp_size + lax.axis_index("fsdp")
    plans = step_plans(dp_size, fsdp_size)
    micro_count = lengths.shape[0]
    token_count, model_width = tokens.shape
    slot_count = token_count // micro_count
    head_size = model_width // HEADS
    hidden_width = w_gate.shape[1]
    width = 4 * head_size
    half_width = model_width // 2
    half_steps = half_width // width
    exchange = partial(Exchange, place=place, device_count=device_count)

    gain_columns = jnp.pad(jnp.stack([gain_one, gain_two], axis=1), ((0, 0), (0, 126)))
    gather = partial(Gather, place=place, device_count=device_count)
    projections = (w_query, w_key, w_value)
    first_set = lax.all_gather(
        jnp.concatenate([*projections, gain_columns], axis=1), AXES, axis=0, tiled=True
    )
    second_set = lax.all_gather(
        jnp.concatenate([w_gate, w_up], axis=1), AXES, axis=0, tiled=True
    )
    out_rows = gather(w_out, plans["gather"])
    down_rows = gather(w_down, plans["gather"])

    inputs = tokens.astype(jnp.float32)
    layouts = [bucket_layout(lengths[index], slot_count) for index in range(micro_count)]
    position = jnp.concatenate([layout[1] for layout in layouts])
    valid = jnp.concatenate([layout[2] for layout in layouts])
    cosine, sine = rope_tables(position, head_size)
    cosine = jnp.tile(cosine, (1, 2 * PAIR // head_size))
    sine = jnp.tile(jnp.concatenate([-sine, sine], axis=1), (1, PAIR // head_size))
    bias = jnp.stack(
        [
            jnp.where(allowed_mask(layout[0], layout[2]).T, 0.0, -1e30).astype(jnp.float32)
            for layout in layouts
        ]
    )
    scale_one = rms_scale(inputs)

    scale_one = tick(scale_one, [], [out_rows, down_rows])
    scale_one = tick(scale_one, [out_rows, down_rows], [out_rows, down_rows])
    gain_first_f = first_set[:, 3 * model_width].astype(jnp.float32)[None, :]
    gain_second_f = first_set[:, 3 * model_width + 1].astype(jnp.float32)[None, :]
    normed = (inputs * scale_one * gain_first_f).astype(jnp.bfloat16)
    query_rot, key_rot, value_mix, context, lse = attend(
        normed, first_set, first_values, bias, cosine, sine, head_size, width
    )
    context = tick(context, [out_rows, down_rows], [out_rows, down_rows])
    while out_rows.steps:
        context = tick(context, [out_rows], [out_rows])
    out_w = out_rows.current
    hidden = inputs + forward_dot(context, out_w)
    scale_two = rms_scale(hidden)
    normed_two = (hidden * scale_two * gain_second_f).astype(jnp.bfloat16)
    gate_w = second_set[:, :hidden_width]
    up_w = second_set[:, hidden_width:]
    while down_rows.steps:
        normed_two = tick(normed_two, [down_rows], [down_rows])
    down_w = down_rows.current
    gate_values = forward_dot(normed_two, gate_w)
    upward = forward_dot(normed_two, up_w)
    sigmoid_gate = jax.nn.sigmoid(gate_values)
    silu_gate = gate_values * sigmoid_gate
    product = (silu_gate * upward).astype(jnp.bfloat16)
    grad_y = cotangent.astype(jnp.float32) * valid.astype(jnp.float32)[:, None]
    grad_y_low = grad_y.astype(jnp.bfloat16)
    down = exchange(
        contract_first(product, grad_y_low).astype(jnp.bfloat16)[None], plans["high_first"]
    )
    grad_y_low = tick(grad_y_low, [], [down])
    grad_product = contract_last(grad_y_low, down_w)
    grad_upward = (grad_product * silu_gate).astype(jnp.bfloat16)
    grad_gate_low = (
        grad_product * upward * sigmoid_gate * (1.0 + gate_values * (1.0 - sigmoid_gate))
    ).astype(jnp.bfloat16)
    grad_upward, grad_gate_low = tick((grad_upward, grad_gate_low), [down], [down])
    gate = exchange(
        contract_first(normed_two, grad_gate_low).astype(jnp.bfloat16)[None], plans["low_first"]
    )
    up = exchange(
        contract_first(normed_two, grad_upward).astype(jnp.bfloat16)[None], plans["high_first"]
    )
    grad_upward, grad_gate_low = tick((grad_upward, grad_gate_low), [], [gate, up])
    grad_normed_two = contract_last(grad_gate_low, gate_w) + contract_last(grad_upward, up_w)
    grad_normed_two = tick(grad_normed_two, [gate, up], [gate, up])
    inner_two = grad_normed_two * gain_second_f
    grad_hidden = (
        grad_y
        + scale_two * inner_two
        - hidden * scale_two**3 * jnp.mean(inner_two * hidden, axis=-1, keepdims=True)
    )
    grad_hidden_low = grad_hidden.astype(jnp.bfloat16)
    grad_context = contract_last(grad_hidden_low, out_w).astype(jnp.bfloat16)
    grad_out_w = jnp.stack(
        [
            contract_first(context, grad_hidden_low[:, low : low + half_width])
            for low in (0, half_width)
        ]
    ).astype(jnp.bfloat16)
    grad_context, grad_out_w = tick((grad_context, grad_out_w), [down], [down])

    def attend_back_half(half, grad_context, first):
        return attend_back(
            query_rot,
            key_rot,
            value_mix,
            grad_context,
            lse,
            bias,
            cosine,
            sine,
            head_size,
            width,
            half * half_steps,
            half_steps,
            first,
        )

    def weight_parts(low):
        return [contract_first(normed, low[index]).astype(jnp.bfloat16) for index in range(3)]

    low_one, first_part = attend_back_half(0, grad_context, None)
    low_one, grad_context = tick((low_one, grad_context), [gate, up], [gate, up])
    one = exchange(
        jnp.concatenate([jnp.stack(weight_parts(low_one)), grad_out_w]), plans["short"]
    )
    grad_context, product = tick((grad_context, product), [], [one])
    out_tokens = (hidden + forward_dot(product, down_w)).astype(jnp.bfloat16)
    grad_context, out_tokens = tick((grad_context, out_tokens), [one, down], [one, down])
    low_two, grad_first = attend_back_half(1, grad_context, first_part)
    two = exchange(jnp.stack(weight_parts(low_two)), plans["short"])
    low_one, low_two = tick((low_one, low_two), [], [two])

    def normed_part(low, half):
        return sum(
            contract_last(low[index], first_set[:, start : start + half_width])
            for index in range(3)
            for start in [index * model_width + half * half_width]
        )

    part_one = normed_part(low_one, 0)
    part_one, low_two = tick((part_one, low_two), [two, gate, up, down], [two, gate, up, down])
    grad_normed = part_one + normed_part(low_two, 1)
    grad_normed = tick(grad_normed, [one], [one])
    inner_one = grad_normed * gain_first_f
    grad_tokens = (
        grad_hidden
        + scale_one * inner_one
        - inputs * scale_one**3 * jnp.mean(inner_one * inputs, axis=-1, keepdims=True)
    )
    grad_tokens = tick(grad_tokens, [two], [two])
    pending = [gate, up, down, one, two]
    while True:
        pending = [item for item in pending if item.steps]
        if not pending:
            break
        for item in pending:
            if item.got is not None:
                item.settle(item.got)
            if item.steps:
                item.launch(item.outgoing())
    projection_sums = [
        jnp.concatenate([one.current[index], two.current[index]], axis=1) for index in range(3)
    ]
    grad_out_sum = jnp.concatenate([one.current[3], one.current[4]], axis=1)
    grad_gate_sum = gate.current[0]
    grad_up_sum = up.current[0]
    grad_down_sum = down.current[0]

    def gain_grad(gain, sums, weights):
        total = sum(
            jnp.sum(grads * weight.astype(jnp.float32), axis=1)
            for grads, weight in zip(sums, weights)
        )
        return total / gain.astype(jnp.float32)

    return (
        out_tokens,
        grad_tokens,
        grad_first,
        *projection_sums,
        grad_out_sum,
        grad_gate_sum,
        grad_up_sum,
        grad_down_sum,
        gain_grad(gain_one, projection_sums, projections),
        gain_grad(gain_two, (grad_gate_sum, grad_up_sum), (w_gate, w_up)),
    )


def solution(mesh):
    rows = P(AXES, None)
    ends = P(AXES)
    return jax.shard_map(
        partial(shards, mesh.shape["dp"], mesh.shape["fsdp"]),
        mesh=mesh,
        in_specs=(rows,) * 11 + (ends,) * 2,
        out_specs=(rows,) * 10 + (ends,) * 2,
        check_vma=False,
    )
```

```python
import math
from functools import partial

import jax
import jax.numpy as jnp
from jax import lax
from jax.experimental import pallas as pl
from jax.experimental.pallas import tpu as pltpu
from jax.sharding import PartitionSpec as P

HEADS = 16


EPSILON = 1e-06


def forward_dot(left, right):
    return jnp.dot(left, right, preferred_element_type=jnp.float32)


def contract_last(left, right):
    return lax.dot_general(
        left, right, (((1,), (1,)), ((), ())), preferred_element_type=jnp.float32
    )


def contract_first(left, right):
    return lax.dot_general(
        left, right, (((0,), (0,)), ((), ())), preferred_element_type=jnp.float32
    )


def bucket_layout(lengths_row, slot_count):
    seq_ends = jnp.cumsum(lengths_row)
    slot_places = jnp.arange(slot_count, dtype=jnp.int32)
    ended_mask = seq_ends[None, :] <= slot_places[:, None]
    segment = jnp.sum(ended_mask.astype(jnp.int32), axis=1)
    before_total = jnp.sum(jnp.where(ended_mask, lengths_row[None, :], 0), axis=1)
    return (segment, slot_places - before_total, slot_places < seq_ends[-1])


def rope_tables(position, head_size):
    half_size = head_size // 2
    frequency = jnp.exp(
        jnp.arange(half_size, dtype=jnp.float32) * (-2.0 * math.log(10000.0) / head_size)
    )
    angles = position.astype(jnp.float32)[:, None] * frequency[None, :]
    return (jnp.cos(angles), jnp.sin(angles))


def allowed_mask(segment, valid):
    slot_places = jnp.arange(segment.shape[0])
    earlier = slot_places[None, :] < slot_places[:, None]
    same_seq = segment[:, None] == segment[None, :]
    diagonal = slot_places[None, :] == slot_places[:, None]
    return diagonal | same_seq & earlier & valid[:, None]


def rms_scale(matrix):
    return lax.rsqrt(jnp.mean(matrix * matrix, axis=-1, keepdims=True) + EPSILON)


PAIR = 128


def swap_halves(matrix, half_size):
    lane = lax.broadcasted_iota(jnp.int32, matrix.shape, 1)
    first = lane % (2 * half_size) < half_size
    width = matrix.shape[1]
    return jnp.where(
        first, pltpu.roll(matrix, width - half_size, 1), pltpu.roll(matrix, half_size, 1)
    )


def head_part(matrix, head, head_size):
    lane = lax.broadcasted_iota(jnp.int32, matrix.shape, 1)
    return jnp.where(lane // head_size == head, matrix, jnp.zeros_like(matrix))


def attend_kernel(
    slot_count,
    head_size,
    normed_ref,
    wq_ref,
    wk_ref,
    wv_ref,
    first_ref,
    bias_ref,
    cos_ref,
    sin_ref,
    q_ref,
    k_ref,
    v_ref,
    ctx_ref,
    lse_ref,
):
    half_size = head_size // 2
    score_scale = head_size ** (-0.5)
    width = q_ref.shape[1]
    bucket_count = bias_ref.shape[0]
    query_rows = slot_count // 2
    normed = normed_ref[...]
    cosine = cos_ref[...]
    sine = sin_ref[...]
    for raw_ref, w_ref in ((q_ref, wq_ref), (k_ref, wk_ref)):
        raw = forward_dot(normed, w_ref[...])
        for low in range(0, width, PAIR):
            part = raw[:, low : low + PAIR]
            raw_ref[:, low : low + PAIR] = (
                part * cosine + swap_halves(part, half_size) * sine
            ).astype(jnp.bfloat16)
    v_ref[...] = (
        0.5 * forward_dot(normed, wv_ref[...]) + 0.5 * first_ref[...].astype(jnp.float32)
    ).astype(jnp.bfloat16)
    for bucket in range(bucket_count):
        base = bucket * slot_count
        for low in range(0, width, PAIR):
            keys = k_ref[base : base + slot_count, low : low + PAIR]
            queries = q_ref[base : base + slot_count, low : low + PAIR] * score_scale
            values_t = v_ref[base : base + slot_count, low : low + PAIR].T
            for start in range(0, slot_count, query_rows):
                end = start + query_rows
                parts = []
                for head in range(PAIR // head_size):
                    key_head = head_part(keys[:end], head, head_size)
                    scores = (
                        contract_last(key_head, queries[start:end])
                        + bias_ref[bucket, :end, start:end]
                    )
                    top = jnp.max(scores, axis=0, keepdims=True)
                    weights = jnp.exp(scores - top)
                    mass = jnp.sum(weights, axis=0, keepdims=True)
                    row = (low // head_size) + head
                    lse_ref[bucket, 0, row : row + 1, start:end] = top + jnp.log(mass)
                    mixed = forward_dot(
                        values_t[head * head_size : (head + 1) * head_size, :end],
                        weights.astype(jnp.bfloat16),
                    )
                    parts.append(mixed * (1.0 / mass))
                ctx_ref[base + start : base + end, low : low + PAIR] = (
                    jnp.concatenate(parts, axis=0).T.astype(jnp.bfloat16)
                )


def attend(normed, weights, first_values, bias, cosine, sine, head_size, width):
    token_count, model_width = normed.shape
    bucket_count, slot_count = bias.shape[:2]
    steps = model_width // width
    whole = lambda step: (0, 0)
    block = pl.BlockSpec((token_count, width), lambda step: (0, step))
    heads = width // head_size
    table = pl.BlockSpec((token_count, PAIR), whole)
    low_shape = jax.ShapeDtypeStruct((token_count, steps * width), jnp.bfloat16)
    return pl.pallas_call(
        partial(attend_kernel, slot_count, head_size),
        grid=(steps,),
        in_specs=[
            pl.BlockSpec((token_count, model_width), whole),
            pl.BlockSpec((model_width, width), lambda step: (0, step)),
            pl.BlockSpec((model_width, width), lambda step: (0, steps + step)),
            pl.BlockSpec((model_width, width), lambda step: (0, 2 * steps + step)),
            block,
            pl.BlockSpec((bucket_count, slot_count, slot_count), lambda step: (0, 0, 0)),
            table,
            table,
        ],
        out_specs=[
            block,
            block,
            block,
            block,
            pl.BlockSpec((bucket_count, 1, heads, slot_count), lambda step: (0, step, 0, 0)),
        ],
        out_shape=[low_shape] * 4
        + [jax.ShapeDtypeStruct((bucket_count, steps, heads, slot_count), jnp.float32)],
        compiler_params=pltpu.CompilerParams(vmem_limit_bytes=56 << 20),
        name="attend",
    )(normed, weights, weights, weights, first_values, bias, cosine, sine)


def attend_back_kernel(
    slot_count,
    head_size,
    q_ref,
    k_ref,
    v_ref,
    grad_ref,
    lse_ref,
    bias_ref,
    cos_ref,
    sin_ref,
    *rest,
):
    normed_t_ref = rest[0]
    grads_ref, first_ref, weights_ref, dk_ref, dv_ref = rest[-5:]
    half_size = head_size // 2
    score_scale = head_size ** (-0.5)
    width = q_ref.shape[1]
    bucket_count = bias_ref.shape[0]
    query_rows = slot_count // 2
    head_count = PAIR // head_size
    for bucket in range(bucket_count):
        base = bucket * slot_count
        cosine = cos_ref[base : base + slot_count]
        sine = sin_ref[base : base + slot_count]
        for low in range(0, width, PAIR):
            keys = k_ref[base : base + slot_count, low : low + PAIR]
            values = v_ref[base : base + slot_count, low : low + PAIR]
            queries = q_ref[base : base + slot_count, low : low + PAIR] * score_scale
            grads = grad_ref[base : base + slot_count, low : low + PAIR]
            keys_t = keys.T
            query_parts = []
            for start in range(0, slot_count, query_rows):
                end = start + query_rows
                parts = []
                for head in range(head_count):
                    row = (low // head_size) + head
                    scores = contract_last(
                        head_part(keys[:end], head, head_size), queries[start:end]
                    )
                    probs = jnp.exp(
                        scores
                        + bias_ref[bucket, :end, start:end]
                        - lse_ref[bucket, 0, row : row + 1, start:end]
                    )
                    grad_probs = contract_last(
                        head_part(values[:end], head, head_size), grads[start:end]
                    )
                    weighted = probs * grad_probs
                    grad_scores = (
                        weighted - probs * jnp.sum(weighted, axis=0, keepdims=True)
                    ).astype(jnp.bfloat16)
                    dv = forward_dot(probs.astype(jnp.bfloat16), grads[start:end])
                    dk = forward_dot(grad_scores, queries[start:end])
                    if start == 0:
                        dv_ref[head, :end] = dv
                        dk_ref[head, :end] = dk
                    else:
                        dv_ref[head, :start] += dv[:start]
                        dk_ref[head, :start] += dk[:start]
                        dv_ref[head, start:end] = dv[start:]
                        dk_ref[head, start:end] = dk[start:]
                    parts.append(
                        forward_dot(
                            keys_t[head * head_size : (head + 1) * head_size, :end], grad_scores
                        )
                    )
                query_parts.append((jnp.concatenate(parts, axis=0) * score_scale).T)
            lane = lax.broadcasted_iota(jnp.int32, (slot_count, PAIR), 1)
            dv = dv_ref[0]
            dk = dk_ref[0]
            for head in range(1, head_count):
                here = lane // head_size == head
                dv = jnp.where(here, dv_ref[head], dv)
                dk = jnp.where(here, dk_ref[head], dk)
            dq = jnp.concatenate(query_parts, axis=0)
            rows = slice(base, base + slot_count)
            for index, part in enumerate((dq, dk)):
                grads_ref[index, rows, low : low + PAIR] = (
                    part * cosine - swap_halves(part, half_size) * sine
                ).astype(jnp.bfloat16)
            first_ref[rows, low : low + PAIR] = 0.5 * dv
            grads_ref[2, rows, low : low + PAIR] = (0.5 * dv).astype(jnp.bfloat16)
    for index in range(3):
        weights_ref[index] = forward_dot(normed_t_ref[...], grads_ref[index]).astype(jnp.bfloat16)


def attend_back(
    queries,
    keys,
    values,
    grads,
    lse,
    bias,
    cosine,
    sine,
    normed_t,
    head_size,
    width,
    first_step,
    steps,
    first,
):
    token_count, model_width = queries.shape
    bucket_count, slot_count = bias.shape[:2]
    heads = width // head_size
    block = pl.BlockSpec((token_count, width), lambda step: (0, first_step + step))
    table = pl.BlockSpec((token_count, PAIR), lambda step: (0, 0))
    shared = [] if first is None else [first]
    return pl.pallas_call(
        partial(attend_back_kernel, slot_count, head_size),
        grid=(steps,),
        in_specs=[
            block,
            block,
            block,
            block,
            pl.BlockSpec(
                (bucket_count, 1, heads, slot_count), lambda step: (0, first_step + step, 0, 0)
            ),
            pl.BlockSpec((bucket_count, slot_count, slot_count), lambda step: (0, 0, 0)),
            table,
            table,
            pl.BlockSpec((model_width, token_count), lambda step: (0, 0)),
        ]
        + [pl.BlockSpec(memory_space=pl.ANY)] * len(shared),
        out_specs=[
            pl.BlockSpec((3, token_count, width), lambda step: (0, 0, step)),
            block,
            pl.BlockSpec((3, model_width, width), lambda step: (0, 0, step)),
        ],
        out_shape=[
            jax.ShapeDtypeStruct((3, token_count, steps * width), jnp.bfloat16),
            jax.ShapeDtypeStruct((token_count, model_width), jnp.float32),
            jax.ShapeDtypeStruct((3, model_width, steps * width), jnp.bfloat16),
        ],
        scratch_shapes=[
            pltpu.VMEM((PAIR // head_size, slot_count, PAIR), jnp.float32),
            pltpu.VMEM((PAIR // head_size, slot_count, PAIR), jnp.float32),
        ],
        input_output_aliases={9: 1} if shared else {},
        compiler_params=pltpu.CompilerParams(vmem_limit_bytes=56 << 20),
        cost_estimate=pl.CostEstimate(flops=1, transcendentals=0, bytes_accessed=1),
        name="attend_back",
    )(queries, keys, values, grads, lse, bias, cosine, sine, normed_t, *shared)


def finish_kernel(
    low_one_ref,
    low_two_ref,
    wq_ref,
    wk_ref,
    wv_ref,
    hidden_ref,
    x_ref,
    scale_ref,
    gain_ref,
    out_ref,
):
    half = low_one_ref.shape[2]
    total = None
    for index, w_ref in enumerate((wq_ref, wk_ref, wv_ref)):
        for low_ref, start in ((low_one_ref, 0), (low_two_ref, half)):
            part = contract_last(low_ref[index], w_ref[:, start : start + half])
            total = part if total is None else total + part
    inner = total * gain_ref[...]
    inputs = x_ref[...].astype(jnp.float32)
    scale = scale_ref[...]
    mean = jnp.mean(inner * inputs, axis=-1, keepdims=True)
    out_ref[...] = hidden_ref[...] + scale * inner - inputs * scale**3 * mean


def finish(low_one, low_two, weights, grad_hidden, inputs, scale, gain):
    token_count, model_width = inputs.shape
    rows = token_count // 4
    row_block = pl.BlockSpec((rows, model_width), lambda step: (step, 0))
    low_block = pl.BlockSpec((3, rows, model_width // 2), lambda step: (0, step, 0))
    weight_blocks = [
        pl.BlockSpec((model_width, model_width), lambda step, index=index: (0, index))
        for index in range(3)
    ]
    return pl.pallas_call(
        finish_kernel,
        grid=(4,),
        in_specs=[low_block, low_block]
        + weight_blocks
        + [
            row_block,
            row_block,
            pl.BlockSpec((rows, 1), lambda step: (step, 0)),
            pl.BlockSpec((1, model_width), lambda step: (0, 0)),
        ],
        out_specs=row_block,
        out_shape=jax.ShapeDtypeStruct((token_count, model_width), jnp.float32),
        compiler_params=pltpu.CompilerParams(vmem_limit_bytes=56 << 20),
        cost_estimate=pl.CostEstimate(flops=1, transcendentals=0, bytes_accessed=1),
        name="finish",
    )(low_one, low_two, weights, weights, weights, grad_hidden, inputs, scale, gain)


AXES = ("dp", "fsdp")


def flip(value, mask, device_count):
    pairs = [(place, place ^ mask) for place in range(device_count)]
    return lax.ppermute(value, AXES, pairs)


def masks_of(bits):
    masks = [0]
    for bit in bits:
        masks += [mask | 1 << bit for mask in masks]
    return masks


class Exchange:
    def __init__(self, partial_sum, steps, place, device_count):
        self.current = partial_sum
        self.steps = [list(step) for step in steps]
        self.left = sorted([bit for step in steps for bit in step], reverse=True)
        self.place = place
        self.device_count = device_count
        self.got = None

    def part(self, mask):
        value = self.current
        left = list(self.left)
        for bit in self.steps[0]:
            lead, row_count, width = value.shape
            high = 1 << left.index(bit)
            view = value.reshape(lead, high, 2, row_count // (2 * high), width)
            chosen = ((self.place ^ mask) >> bit) & 1
            value = lax.dynamic_index_in_dim(view, chosen, 2, keepdims=False)
            value = value.reshape(lead, row_count // 2, width)
            left.remove(bit)
        return value

    def outgoing(self):
        masks = masks_of(self.steps[0])
        self.kept = self.part(0)
        return [self.part(mask) for mask in masks[1:]]

    def launch(self, sent):
        masks = masks_of(self.steps[0])[1:]
        self.got = [flip(value, mask, self.device_count) for value, mask in zip(sent, masks)]

    def settle(self, got):
        total = self.kept.astype(jnp.float32)
        for value in got:
            total = total + value.astype(jnp.float32)
        for bit in self.steps.pop(0):
            self.left.remove(bit)
        self.current = total.astype(jnp.bfloat16) if self.steps else total


class Gather:
    def __init__(self, rows, steps, place, device_count):
        self.current = rows
        self.steps = [list(step) for step in steps]
        self.have = []
        self.place = place
        self.device_count = device_count
        self.got = None

    def outgoing(self):
        return [self.current]

    def launch(self, sent):
        masks = masks_of(self.steps[0])[1:]
        self.got = [flip(sent[0], mask, self.device_count) for mask in masks]

    def settle(self, got):
        pieces = [self.current] + list(got)
        for bit in self.steps.pop(0):
            row_count, width = pieces[0].shape
            high = 1 << len([other for other in self.have if other > bit])
            shape = (high, 1, row_count // high, width)
            side = lax.broadcasted_iota(jnp.int32, (1, 2, 1, 1), 1)
            mine = side == ((self.place >> bit) & 1)
            pieces = [
                jnp.where(mine, near.reshape(shape), far.reshape(shape)).reshape(
                    2 * row_count, width
                )
                for near, far in zip(pieces[0::2], pieces[1::2])
            ]
            self.have.append(bit)
        self.current = pieces[0]


def tick(chain, settled, launched):
    settled = [item for item in settled if item.got is not None]
    if settled:
        chain, gots = lax.optimization_barrier((chain, [item.got for item in settled]))
        for item, got in zip(settled, gots):
            item.settle(got)
            item.got = None
    launched = [item for item in launched if item.steps and item.got is None]
    if launched:
        chain, sents = lax.optimization_barrier((chain, [item.outgoing() for item in launched]))
        for item, sent in zip(launched, sents):
            item.launch(sent)
    return chain


def step_plans(dp_size, fsdp_size):
    bit_count = (dp_size * fsdp_size).bit_length() - 1
    core_bit = fsdp_size.bit_length() - 1
    high = list(range(core_bit + 1, bit_count))
    rest = list(range(1, core_bit))
    pairs = [rest[index : index + 2] for index in range(0, len(rest), 2)]
    core = [core_bit]
    singles = [[bit] for bit in rest]
    return {
        "high_first": [core, high, [0]] + singles,
        "low_first": [core, [0], high] + singles,
        "short": [core, high + [0]] + pairs,
        "gather": pairs[::-1] + [[0] + high, core],
    }


def shards(
    dp_size,
    fsdp_size,
    tokens,
    first_values,
    cotangent,
    lengths,
    w_query,
    w_key,
    w_value,
    w_out,
    w_gate,
    w_up,
    w_down,
    gain_one,
    gain_two,
):
    device_count = dp_size * fsdp_size
    place = lax.axis_index("dp") * fsdp_size + lax.axis_index("fsdp")
    plans = step_plans(dp_size, fsdp_size)
    micro_count = lengths.shape[0]
    token_count, model_width = tokens.shape
    slot_count = token_count // micro_count
    head_size = model_width // HEADS
    hidden_width = w_gate.shape[1]
    width = 4 * head_size
    half_width = model_width // 2
    half_steps = half_width // width
    exchange = partial(Exchange, place=place, device_count=device_count)

    gain_columns = jnp.pad(jnp.stack([gain_one, gain_two], axis=1), ((0, 0), (0, 126)))
    gather = partial(Gather, place=place, device_count=device_count)
    projections = (w_query, w_key, w_value)
    first_set = lax.all_gather(
        jnp.concatenate([*projections, gain_columns], axis=1), AXES, axis=0, tiled=True
    )
    second_set = lax.all_gather(
        jnp.concatenate([w_gate, w_up], axis=1), AXES, axis=0, tiled=True
    )
    out_rows = gather(w_out, plans["gather"])
    down_rows = gather(w_down, plans["gather"])

    inputs = tokens.astype(jnp.float32)
    layouts = [bucket_layout(lengths[index], slot_count) for index in range(micro_count)]
    position = jnp.concatenate([layout[1] for layout in layouts])
    valid = jnp.concatenate([layout[2] for layout in layouts])
    cosine, sine = rope_tables(position, head_size)
    cosine = jnp.tile(cosine, (1, 2 * PAIR // head_size))
    sine = jnp.tile(jnp.concatenate([-sine, sine], axis=1), (1, PAIR // head_size))
    bias = jnp.stack(
        [
            jnp.where(allowed_mask(layout[0], layout[2]).T, 0.0, -1e30).astype(jnp.float32)
            for layout in layouts
        ]
    )
    scale_one = rms_scale(inputs)

    scale_one = tick(scale_one, [], [out_rows, down_rows])
    scale_one = tick(scale_one, [out_rows, down_rows], [out_rows])
    scale_one = tick(scale_one, [out_rows], [])
    gain_first_f = first_set[:, 3 * model_width].astype(jnp.float32)[None, :]
    gain_second_f = first_set[:, 3 * model_width + 1].astype(jnp.float32)[None, :]
    normed = (inputs * scale_one * gain_first_f).astype(jnp.bfloat16)
    normed = tick(normed, [], [out_rows, down_rows])
    query_rot, key_rot, value_mix, context, lse = attend(
        normed, first_set, first_values, bias, cosine, sine, head_size, width
    )
    context = tick(context, [out_rows, down_rows], [out_rows, down_rows])
    while out_rows.steps:
        context = tick(context, [out_rows], [out_rows])
    out_w = out_rows.current
    hidden = inputs + forward_dot(context, out_w)
    scale_two = rms_scale(hidden)
    normed_two = (hidden * scale_two * gain_second_f).astype(jnp.bfloat16)
    gate_w = second_set[:, :hidden_width]
    up_w = second_set[:, hidden_width:]
    while down_rows.steps:
        normed_two = tick(normed_two, [down_rows], [down_rows])
    down_w = down_rows.current
    grad_y = cotangent.astype(jnp.float32) * valid.astype(jnp.float32)[:, None]
    grad_y_low = grad_y.astype(jnp.bfloat16)
    grad_product = contract_last(grad_y_low, down_w)
    normed_two, grad_product = lax.optimization_barrier((normed_two, grad_product))
    gate_values = forward_dot(normed_two, gate_w)
    upward = forward_dot(normed_two, up_w)
    sigmoid_gate = jax.nn.sigmoid(gate_values)
    silu_gate = gate_values * sigmoid_gate
    product = (silu_gate * upward).astype(jnp.bfloat16)
    grad_upward = (grad_product * silu_gate).astype(jnp.bfloat16)
    grad_gate_low = (
        grad_product * upward * sigmoid_gate * (1.0 + gate_values * (1.0 - sigmoid_gate))
    ).astype(jnp.bfloat16)
    gate = exchange(
        contract_first(normed_two, grad_gate_low).astype(jnp.bfloat16)[None], plans["low_first"]
    )
    up = exchange(
        contract_first(normed_two, grad_upward).astype(jnp.bfloat16)[None], plans["high_first"]
    )
    down = exchange(
        contract_first(product, grad_y_low).astype(jnp.bfloat16)[None], plans["high_first"]
    )
    grad_upward, grad_gate_low = tick((grad_upward, grad_gate_low), [], [gate, up, down])
    grad_normed_two = contract_last(grad_gate_low, gate_w) + contract_last(grad_upward, up_w)
    grad_normed_two = tick(grad_normed_two, [gate, up, down], [gate, up])
    inner_two = grad_normed_two * gain_second_f
    grad_hidden = (
        grad_y
        + scale_two * inner_two
        - hidden * scale_two**3 * jnp.mean(inner_two * hidden, axis=-1, keepdims=True)
    )
    grad_hidden_low = grad_hidden.astype(jnp.bfloat16)
    grad_context = contract_last(grad_hidden_low, out_w).astype(jnp.bfloat16)
    grad_out_w = jnp.stack(
        [
            contract_first(context, grad_hidden_low[:, low : low + half_width])
            for low in (0, half_width)
        ]
    ).astype(jnp.bfloat16)
    normed_t = normed.T
    grad_context, grad_out_w, normed_t = lax.optimization_barrier(
        (grad_context, grad_out_w, normed_t)
    )

    def attend_back_half(half, grad_context, first):
        return attend_back(
            query_rot,
            key_rot,
            value_mix,
            grad_context,
            lse,
            bias,
            cosine,
            sine,
            normed_t,
            head_size,
            width,
            half * half_steps,
            half_steps,
            first,
        )

    low_one, first_part, weights_one = attend_back_half(0, grad_context, None)
    one = exchange(jnp.concatenate([weights_one, grad_out_w]), plans["low_first"])
    grad_context, product = tick((grad_context, product), [gate, up], [gate, up, one])
    out_tokens = (hidden + forward_dot(product, down_w)).astype(jnp.bfloat16)
    grad_context, out_tokens = tick(
        (grad_context, out_tokens), [gate, up, one], [down, one, gate, up]
    )
    low_two, grad_first, weights_two = attend_back_half(1, grad_context, first_part)
    two = exchange(weights_two, plans["short"])
    low_two = tick(low_two, [down, one, gate, up], [two, down, one, gate, up])
    grad_tokens = finish(
        low_one, low_two, first_set, grad_hidden, tokens, scale_one, gain_first_f
    )
    grad_tokens = tick(grad_tokens, [two, down, one, gate, up], [two, down, one])
    pending = [two, down, one, gate, up]
    while any(item.steps for item in pending):
        grad_tokens = tick(grad_tokens, pending, pending)
    projection_sums = [
        jnp.concatenate([one.current[index], two.current[index]], axis=1) for index in range(3)
    ]
    grad_out_sum = jnp.concatenate([one.current[3], one.current[4]], axis=1)
    grad_gate_sum = gate.current[0]
    grad_up_sum = up.current[0]
    grad_down_sum = down.current[0]

    def gain_grad(gain, sums, weights):
        total = sum(
            jnp.sum(grads * weight.astype(jnp.float32), axis=1)
            for grads, weight in zip(sums, weights)
        )
        return total / gain.astype(jnp.float32)

    return (
        out_tokens,
        grad_tokens,
        grad_first,
        *projection_sums,
        grad_out_sum,
        grad_gate_sum,
        grad_up_sum,
        grad_down_sum,
        gain_grad(gain_one, projection_sums, projections),
        gain_grad(gain_two, (grad_gate_sum, grad_up_sum), (w_gate, w_up)),
    )


def solution(mesh):
    rows = P(AXES, None)
    ends = P(AXES)
    return jax.shard_map(
        partial(shards, mesh.shape["dp"], mesh.shape["fsdp"]),
        mesh=mesh,
        in_specs=(rows,) * 11 + (ends,) * 2,
        out_specs=(rows,) * 10 + (ends,) * 2,
        check_vma=False,
    )
```

```python
import math
from functools import partial

import jax
import jax.numpy as jnp
from jax import lax
from jax.experimental import pallas as pl
from jax.experimental.pallas import tpu as pltpu
from jax.sharding import PartitionSpec as P

HEADS = 16


EPSILON = 1e-06


def forward_dot(left, right):
    return jnp.dot(left, right, preferred_element_type=jnp.float32)


def contract_last(left, right):
    return lax.dot_general(
        left, right, (((1,), (1,)), ((), ())), preferred_element_type=jnp.float32
    )


def contract_first(left, right):
    return lax.dot_general(
        left, right, (((0,), (0,)), ((), ())), preferred_element_type=jnp.float32
    )


def bucket_layout(lengths_row, slot_count):
    seq_ends = jnp.cumsum(lengths_row)
    slot_places = jnp.arange(slot_count, dtype=jnp.int32)
    ended_mask = seq_ends[None, :] <= slot_places[:, None]
    segment = jnp.sum(ended_mask.astype(jnp.int32), axis=1)
    before_total = jnp.sum(jnp.where(ended_mask, lengths_row[None, :], 0), axis=1)
    return (segment, slot_places - before_total, slot_places < seq_ends[-1])


def rope_tables(position, head_size):
    half_size = head_size // 2
    frequency = jnp.exp(
        jnp.arange(half_size, dtype=jnp.float32) * (-2.0 * math.log(10000.0) / head_size)
    )
    angles = position.astype(jnp.float32)[:, None] * frequency[None, :]
    return (jnp.cos(angles), jnp.sin(angles))


def allowed_mask(segment, valid):
    slot_places = jnp.arange(segment.shape[0])
    earlier = slot_places[None, :] < slot_places[:, None]
    same_seq = segment[:, None] == segment[None, :]
    diagonal = slot_places[None, :] == slot_places[:, None]
    return diagonal | same_seq & earlier & valid[:, None]


def rms_scale(matrix):
    return lax.rsqrt(jnp.mean(matrix * matrix, axis=-1, keepdims=True) + EPSILON)


PAIR = 128


def swap_halves(matrix, half_size):
    lane = lax.broadcasted_iota(jnp.int32, matrix.shape, 1)
    first = lane % (2 * half_size) < half_size
    width = matrix.shape[1]
    return jnp.where(
        first, pltpu.roll(matrix, width - half_size, 1), pltpu.roll(matrix, half_size, 1)
    )


def head_part(matrix, head, head_size):
    lane = lax.broadcasted_iota(jnp.int32, matrix.shape, 1)
    return jnp.where(lane // head_size == head, matrix, jnp.zeros_like(matrix))


def attend_kernel(
    slot_count,
    head_size,
    normed_ref,
    wq_ref,
    wk_ref,
    wv_ref,
    first_ref,
    bias_ref,
    cos_ref,
    sin_ref,
    q_ref,
    k_ref,
    v_ref,
    ctx_ref,
    lse_ref,
):
    half_size = head_size // 2
    score_scale = head_size ** (-0.5)
    width = q_ref.shape[1]
    bucket_count = bias_ref.shape[0]
    query_rows = slot_count // 2
    normed = normed_ref[...]
    cosine = cos_ref[...]
    sine = sin_ref[...]
    for raw_ref, w_ref in ((q_ref, wq_ref), (k_ref, wk_ref)):
        raw = forward_dot(normed, w_ref[...])
        for low in range(0, width, PAIR):
            part = raw[:, low : low + PAIR]
            raw_ref[:, low : low + PAIR] = (
                part * cosine + swap_halves(part, half_size) * sine
            ).astype(jnp.bfloat16)
    v_ref[...] = (
        0.5 * forward_dot(normed, wv_ref[...]) + 0.5 * first_ref[...].astype(jnp.float32)
    ).astype(jnp.bfloat16)
    for bucket in range(bucket_count):
        base = bucket * slot_count
        for low in range(0, width, PAIR):
            keys = k_ref[base : base + slot_count, low : low + PAIR]
            queries = q_ref[base : base + slot_count, low : low + PAIR] * score_scale
            values_t = v_ref[base : base + slot_count, low : low + PAIR].T
            for start in range(0, slot_count, query_rows):
                end = start + query_rows
                parts = []
                for head in range(PAIR // head_size):
                    key_head = head_part(keys[:end], head, head_size)
                    scores = (
                        contract_last(key_head, queries[start:end])
                        + bias_ref[bucket, :end, start:end]
                    )
                    top = jnp.max(scores, axis=0, keepdims=True)
                    weights = jnp.exp(scores - top)
                    mass = jnp.sum(weights, axis=0, keepdims=True)
                    row = (low // head_size) + head
                    lse_ref[bucket, 0, row : row + 1, start:end] = top + jnp.log(mass)
                    mixed = forward_dot(
                        values_t[head * head_size : (head + 1) * head_size, :end],
                        weights.astype(jnp.bfloat16),
                    )
                    parts.append(mixed * (1.0 / mass))
                ctx_ref[base + start : base + end, low : low + PAIR] = (
                    jnp.concatenate(parts, axis=0).T.astype(jnp.bfloat16)
                )


def attend(normed, weights, first_values, bias, cosine, sine, head_size, width):
    token_count, model_width = normed.shape
    bucket_count, slot_count = bias.shape[:2]
    steps = model_width // width
    whole = lambda step: (0, 0)
    block = pl.BlockSpec((token_count, width), lambda step: (0, step))
    heads = width // head_size
    table = pl.BlockSpec((token_count, PAIR), whole)
    low_shape = jax.ShapeDtypeStruct((token_count, steps * width), jnp.bfloat16)
    return pl.pallas_call(
        partial(attend_kernel, slot_count, head_size),
        grid=(steps,),
        in_specs=[
            pl.BlockSpec((token_count, model_width), whole),
            pl.BlockSpec((model_width, width), lambda step: (0, step)),
            pl.BlockSpec((model_width, width), lambda step: (0, steps + step)),
            pl.BlockSpec((model_width, width), lambda step: (0, 2 * steps + step)),
            block,
            pl.BlockSpec((bucket_count, slot_count, slot_count), lambda step: (0, 0, 0)),
            table,
            table,
        ],
        out_specs=[
            block,
            block,
            block,
            block,
            pl.BlockSpec((bucket_count, 1, heads, slot_count), lambda step: (0, step, 0, 0)),
        ],
        out_shape=[low_shape] * 4
        + [jax.ShapeDtypeStruct((bucket_count, steps, heads, slot_count), jnp.float32)],
        compiler_params=pltpu.CompilerParams(vmem_limit_bytes=56 << 20),
        name="attend",
    )(normed, weights, weights, weights, first_values, bias, cosine, sine)


def attend_back_kernel(
    slot_count,
    head_size,
    q_ref,
    k_ref,
    v_ref,
    grad_ref,
    lse_ref,
    bias_ref,
    cos_ref,
    sin_ref,
    *rest,
):
    normed_t_ref = rest[0]
    grads_ref, first_ref, kept_ref, sent_ref, dk_ref, dv_ref = rest[-6:]
    half_size = head_size // 2
    score_scale = head_size ** (-0.5)
    width = q_ref.shape[1]
    bucket_count = bias_ref.shape[0]
    query_rows = slot_count // 2
    head_count = PAIR // head_size
    for bucket in range(bucket_count):
        base = bucket * slot_count
        cosine = cos_ref[base : base + slot_count]
        sine = sin_ref[base : base + slot_count]
        for low in range(0, width, PAIR):
            keys = k_ref[base : base + slot_count, low : low + PAIR]
            values = v_ref[base : base + slot_count, low : low + PAIR]
            queries = q_ref[base : base + slot_count, low : low + PAIR] * score_scale
            grads = grad_ref[base : base + slot_count, low : low + PAIR]
            keys_t = keys.T
            query_parts = []
            for start in range(0, slot_count, query_rows):
                end = start + query_rows
                parts = []
                for head in range(head_count):
                    row = (low // head_size) + head
                    scores = contract_last(
                        head_part(keys[:end], head, head_size), queries[start:end]
                    )
                    probs = jnp.exp(
                        scores
                        + bias_ref[bucket, :end, start:end]
                        - lse_ref[bucket, 0, row : row + 1, start:end]
                    )
                    grad_probs = contract_last(
                        head_part(values[:end], head, head_size), grads[start:end]
                    )
                    weighted = probs * grad_probs
                    grad_scores = (
                        weighted - probs * jnp.sum(weighted, axis=0, keepdims=True)
                    ).astype(jnp.bfloat16)
                    dv = forward_dot(probs.astype(jnp.bfloat16), grads[start:end])
                    dk = forward_dot(grad_scores, queries[start:end])
                    if start == 0:
                        dv_ref[head, :end] = dv
                        dk_ref[head, :end] = dk
                    else:
                        dv_ref[head, :start] += dv[:start]
                        dk_ref[head, :start] += dk[:start]
                        dv_ref[head, start:end] = dv[start:]
                        dk_ref[head, start:end] = dk[start:]
                    parts.append(
                        forward_dot(
                            keys_t[head * head_size : (head + 1) * head_size, :end], grad_scores
                        )
                    )
                query_parts.append((jnp.concatenate(parts, axis=0) * score_scale).T)
            lane = lax.broadcasted_iota(jnp.int32, (slot_count, PAIR), 1)
            dv = dv_ref[0]
            dk = dk_ref[0]
            for head in range(1, head_count):
                here = lane // head_size == head
                dv = jnp.where(here, dv_ref[head], dv)
                dk = jnp.where(here, dk_ref[head], dk)
            dq = jnp.concatenate(query_parts, axis=0)
            rows = slice(base, base + slot_count)
            for index, part in enumerate((dq, dk)):
                grads_ref[index, rows, low : low + PAIR] = (
                    part * cosine - swap_halves(part, half_size) * sine
                ).astype(jnp.bfloat16)
            first_ref[rows, low : low + PAIR] = 0.5 * dv
            grads_ref[2, rows, low : low + PAIR] = (0.5 * dv).astype(jnp.bfloat16)
    products = [(normed_t_ref, grads_ref.at[index]) for index in range(3)]
    if kept_ref.shape[0] > 3:
        products += [(rest[1], rest[2]), (rest[1], rest[3])]
    half = kept_ref.shape[1]
    for index, (left_ref, right_ref) in enumerate(products):
        right = right_ref[...]
        kept_ref[index] = forward_dot(left_ref[:half], right).astype(jnp.bfloat16)
        sent_ref[index] = forward_dot(left_ref[half:], right).astype(jnp.bfloat16)


def attend_back(
    queries,
    keys,
    values,
    grads,
    lse,
    bias,
    cosine,
    sine,
    normed_t,
    context_t,
    grad_hidden_low,
    head_size,
    width,
    first_step,
    steps,
    first,
):
    token_count, model_width = queries.shape
    bucket_count, slot_count = bias.shape[:2]
    heads = width // head_size
    block = pl.BlockSpec((token_count, width), lambda step: (0, first_step + step))
    table = pl.BlockSpec((token_count, PAIR), lambda step: (0, 0))
    lead = 3 if context_t is None else 5
    out_args = [] if context_t is None else [context_t, grad_hidden_low, grad_hidden_low]
    shared = [] if first is None else [first]
    return pl.pallas_call(
        partial(attend_back_kernel, slot_count, head_size),
        grid=(steps,),
        in_specs=[
            block,
            block,
            block,
            block,
            pl.BlockSpec(
                (bucket_count, 1, heads, slot_count), lambda step: (0, first_step + step, 0, 0)
            ),
            pl.BlockSpec((bucket_count, slot_count, slot_count), lambda step: (0, 0, 0)),
            table,
            table,
            pl.BlockSpec((model_width, token_count), lambda step: (0, 0)),
            pl.BlockSpec((model_width, token_count), lambda step: (0, 0)),
            pl.BlockSpec((token_count, width), lambda step: (0, step)),
            pl.BlockSpec((token_count, width), lambda step: (0, steps + step)),
        ][: 9 + len(out_args)]
        + [pl.BlockSpec(memory_space=pl.ANY)] * len(shared),
        out_specs=[
            pl.BlockSpec((3, token_count, width), lambda step: (0, 0, step)),
            block,
        ]
        + [pl.BlockSpec((lead, model_width // 2, width), lambda step: (0, 0, step))] * 2,
        out_shape=[
            jax.ShapeDtypeStruct((3, token_count, steps * width), jnp.bfloat16),
            jax.ShapeDtypeStruct((token_count, model_width), jnp.float32),
        ]
        + [jax.ShapeDtypeStruct((lead, model_width // 2, steps * width), jnp.bfloat16)] * 2,
        scratch_shapes=[
            pltpu.VMEM((PAIR // head_size, slot_count, PAIR), jnp.float32),
            pltpu.VMEM((PAIR // head_size, slot_count, PAIR), jnp.float32),
        ],
        input_output_aliases={9 + len(out_args): 1} if shared else {},
        compiler_params=pltpu.CompilerParams(vmem_limit_bytes=56 << 20),
        cost_estimate=pl.CostEstimate(flops=1, transcendentals=0, bytes_accessed=1),
        name="attend_back",
    )(queries, keys, values, grads, lse, bias, cosine, sine, normed_t, *out_args, *shared)


def feed_kernel(
    normed_ref,
    normed_t_ref,
    grad_y_ref,
    grad_product_ref,
    gate_ref,
    up_ref,
    product_ref,
    grad_gate_ref,
    grad_up_ref,
    gate_kept_ref,
    gate_sent_ref,
    up_kept_ref,
    up_sent_ref,
    down_ref,
):
    gate_values = forward_dot(normed_ref[...], gate_ref[...])
    upward = forward_dot(normed_ref[...], up_ref[...])
    grad_product = grad_product_ref[...]
    sigmoid_gate = jax.nn.sigmoid(gate_values)
    silu_gate = gate_values * sigmoid_gate
    product = (silu_gate * upward).astype(jnp.bfloat16)
    product_ref[...] = product
    grad_up_ref[...] = (grad_product * silu_gate).astype(jnp.bfloat16)
    grad_gate_ref[...] = (
        grad_product * upward * sigmoid_gate * (1.0 + gate_values * (1.0 - sigmoid_gate))
    ).astype(jnp.bfloat16)
    half = gate_kept_ref.shape[0]
    for grads_ref, kept_ref, sent_ref in (
        (grad_gate_ref, gate_kept_ref, gate_sent_ref),
        (grad_up_ref, up_kept_ref, up_sent_ref),
    ):
        grads = grads_ref[...]
        kept_ref[...] = forward_dot(normed_t_ref[:half], grads).astype(jnp.bfloat16)
        sent_ref[...] = forward_dot(normed_t_ref[half:], grads).astype(jnp.bfloat16)
    down_ref[...] = forward_dot(product.T, grad_y_ref[...]).astype(jnp.bfloat16)


def feed(normed, normed_t, grad_y, grad_product, weights):
    token_count, model_width = normed.shape
    hidden_width = grad_product.shape[1]
    width = 256
    steps = hidden_width // width
    whole = lambda step: (0, 0)
    wide = pl.BlockSpec((token_count, width), lambda step: (0, step))
    half = pl.BlockSpec((model_width // 2, width), lambda step: (0, step))
    wide_shape = jax.ShapeDtypeStruct((token_count, hidden_width), jnp.bfloat16)
    half_shape = jax.ShapeDtypeStruct((model_width // 2, hidden_width), jnp.bfloat16)
    return pl.pallas_call(
        feed_kernel,
        grid=(steps,),
        in_specs=[
            pl.BlockSpec((token_count, model_width), whole),
            pl.BlockSpec((model_width, token_count), whole),
            pl.BlockSpec((token_count, model_width), whole),
            wide,
            pl.BlockSpec((model_width, width), lambda step: (0, step)),
            pl.BlockSpec((model_width, width), lambda step: (0, steps + step)),
        ],
        out_specs=[wide] * 3
        + [half] * 4
        + [pl.BlockSpec((width, model_width), lambda step: (step, 0))],
        out_shape=[wide_shape] * 3
        + [half_shape] * 4
        + [jax.ShapeDtypeStruct((hidden_width, model_width), jnp.bfloat16)],
        compiler_params=pltpu.CompilerParams(vmem_limit_bytes=56 << 20),
        cost_estimate=pl.CostEstimate(flops=1, transcendentals=0, bytes_accessed=1),
        name="feed",
    )(normed, normed_t, grad_y, grad_product, weights, weights)


def finish_kernel(
    low_one_ref,
    low_two_ref,
    wq_ref,
    wk_ref,
    wv_ref,
    hidden_ref,
    x_ref,
    scale_ref,
    gain_ref,
    out_ref,
):
    half = low_one_ref.shape[2]
    total = None
    for index, w_ref in enumerate((wq_ref, wk_ref, wv_ref)):
        for low_ref, start in ((low_one_ref, 0), (low_two_ref, half)):
            part = contract_last(low_ref[index], w_ref[:, start : start + half])
            total = part if total is None else total + part
    inner = total * gain_ref[...]
    inputs = x_ref[...].astype(jnp.float32)
    scale = scale_ref[...]
    mean = jnp.mean(inner * inputs, axis=-1, keepdims=True)
    out_ref[...] = hidden_ref[...] + scale * inner - inputs * scale**3 * mean


def finish(low_one, low_two, weights, grad_hidden, inputs, scale, gain):
    token_count, model_width = inputs.shape
    rows = token_count // 4
    row_block = pl.BlockSpec((rows, model_width), lambda step: (step, 0))
    low_block = pl.BlockSpec((3, rows, model_width // 2), lambda step: (0, step, 0))
    weight_blocks = [
        pl.BlockSpec((model_width, model_width), lambda step, index=index: (0, index))
        for index in range(3)
    ]
    return pl.pallas_call(
        finish_kernel,
        grid=(4,),
        in_specs=[low_block, low_block]
        + weight_blocks
        + [
            row_block,
            row_block,
            pl.BlockSpec((rows, 1), lambda step: (step, 0)),
            pl.BlockSpec((1, model_width), lambda step: (0, 0)),
        ],
        out_specs=row_block,
        out_shape=jax.ShapeDtypeStruct((token_count, model_width), jnp.float32),
        compiler_params=pltpu.CompilerParams(vmem_limit_bytes=56 << 20),
        cost_estimate=pl.CostEstimate(flops=1, transcendentals=0, bytes_accessed=1),
        name="finish",
    )(low_one, low_two, weights, weights, weights, grad_hidden, inputs, scale, gain)


AXES = ("dp", "fsdp")


def flip(value, mask, device_count):
    pairs = [(place, place ^ mask) for place in range(device_count)]
    return lax.ppermute(value, AXES, pairs)


def masks_of(bits):
    masks = [0]
    for bit in bits:
        masks += [mask | 1 << bit for mask in masks]
    return masks


class Exchange:
    def __init__(self, partial_sum, steps, place, device_count, first=None):
        self.current = partial_sum
        self.first = first
        self.steps = [list(step) for step in steps]
        self.left = sorted([bit for step in steps for bit in step], reverse=True)
        self.place = place
        self.device_count = device_count
        self.got = None

    def part(self, mask):
        value = self.current
        left = list(self.left)
        for bit in self.steps[0]:
            lead, row_count, width = value.shape
            high = 1 << left.index(bit)
            view = value.reshape(lead, high, 2, row_count // (2 * high), width)
            chosen = ((self.place ^ mask) >> bit) & 1
            value = lax.dynamic_index_in_dim(view, chosen, 2, keepdims=False)
            value = value.reshape(lead, row_count // 2, width)
            left.remove(bit)
        return value

    def outgoing(self):
        if self.first is not None:
            self.kept, sent = self.first
            self.first = None
            return [sent]
        masks = masks_of(self.steps[0])
        self.kept = self.part(0)
        return [self.part(mask) for mask in masks[1:]]

    def launch(self, sent):
        masks = masks_of(self.steps[0])[1:]
        self.got = [flip(value, mask, self.device_count) for value, mask in zip(sent, masks)]

    def settle(self, got):
        total = self.kept.astype(jnp.float32)
        for value in got:
            total = total + value.astype(jnp.float32)
        for bit in self.steps.pop(0):
            self.left.remove(bit)
        self.current = total.astype(jnp.bfloat16) if self.steps else total


class Gather:
    def __init__(self, rows, steps, place, device_count):
        self.current = rows
        self.steps = [list(step) for step in steps]
        self.have = []
        self.place = place
        self.device_count = device_count
        self.got = None

    def outgoing(self):
        return [self.current]

    def launch(self, sent):
        masks = masks_of(self.steps[0])[1:]
        self.got = [flip(sent[0], mask, self.device_count) for mask in masks]

    def settle(self, got):
        pieces = [self.current] + list(got)
        for bit in self.steps.pop(0):
            row_count, width = pieces[0].shape
            high = 1 << len([other for other in self.have if other > bit])
            shape = (high, 1, row_count // high, width)
            side = lax.broadcasted_iota(jnp.int32, (1, 2, 1, 1), 1)
            mine = side == ((self.place >> bit) & 1)
            pieces = [
                jnp.where(mine, near.reshape(shape), far.reshape(shape)).reshape(
                    2 * row_count, width
                )
                for near, far in zip(pieces[0::2], pieces[1::2])
            ]
            self.have.append(bit)
        self.current = pieces[0]


def split_columns(matrix, bit, place, device_count):
    row_count, column_count = matrix.shape
    low = (column_count // device_count) << bit
    mine = (place >> bit) & 1
    return [
        jnp.concatenate(
            [
                lax.dynamic_slice(matrix, (0, start + side * low), (row_count, low))
                for start in range(0, column_count, 2 * low)
            ],
            axis=1,
        )
        for side in (mine, 1 - mine)
    ]


def tick(chain, settled, launched):
    settled = [item for item in settled if item.got is not None]
    if settled:
        chain, gots = lax.optimization_barrier((chain, [item.got for item in settled]))
        for item, got in zip(settled, gots):
            item.settle(got)
            item.got = None
    launched = [item for item in launched if item.steps and item.got is None]
    if launched:
        chain, sents = lax.optimization_barrier((chain, [item.outgoing() for item in launched]))
        for item, sent in zip(launched, sents):
            item.launch(sent)
    return chain


def step_plans(dp_size, fsdp_size):
    bit_count = (dp_size * fsdp_size).bit_length() - 1
    core_bit = fsdp_size.bit_length() - 1
    high = list(range(core_bit + 1, bit_count))
    rest = list(range(1, core_bit))
    pairs = [rest[index : index + 2] for index in range(0, len(rest), 2)]
    core = [core_bit]
    singles = [[bit] for bit in rest]
    return {
        "high_first": [core, high, [0]] + singles,
        "low_first": [core, [0], high] + singles,
        "short": [core, high + [0]] + pairs,
        "gather": pairs[::-1] + [[0] + high, core],
    }


def shards(
    dp_size,
    fsdp_size,
    tokens,
    first_values,
    cotangent,
    lengths,
    w_query,
    w_key,
    w_value,
    w_out,
    w_gate,
    w_up,
    w_down,
    gain_one,
    gain_two,
):
    device_count = dp_size * fsdp_size
    place = lax.axis_index("dp") * fsdp_size + lax.axis_index("fsdp")
    plans = step_plans(dp_size, fsdp_size)
    micro_count = lengths.shape[0]
    token_count, model_width = tokens.shape
    slot_count = token_count // micro_count
    head_size = model_width // HEADS
    hidden_width = w_gate.shape[1]
    width = 4 * head_size
    half_width = model_width // 2
    half_steps = half_width // width
    exchange = partial(Exchange, place=place, device_count=device_count)

    gain_columns = jnp.pad(jnp.stack([gain_one, gain_two], axis=1), ((0, 0), (0, 126)))
    gather = partial(Gather, place=place, device_count=device_count)
    projections = (w_query, w_key, w_value)
    first_set = lax.all_gather(
        jnp.concatenate([*projections, gain_columns], axis=1), AXES, axis=0, tiled=True
    )
    second_set = lax.all_gather(
        jnp.concatenate([w_gate, w_up], axis=1), AXES, axis=0, tiled=True
    )
    out_rows = gather(w_out, plans["gather"])
    down_rows = gather(w_down, plans["gather"])

    inputs = tokens.astype(jnp.float32)
    layouts = [bucket_layout(lengths[index], slot_count) for index in range(micro_count)]
    position = jnp.concatenate([layout[1] for layout in layouts])
    valid = jnp.concatenate([layout[2] for layout in layouts])
    cosine, sine = rope_tables(position, head_size)
    cosine = jnp.tile(cosine, (1, 2 * PAIR // head_size))
    sine = jnp.tile(jnp.concatenate([-sine, sine], axis=1), (1, PAIR // head_size))
    bias = jnp.stack(
        [
            jnp.where(allowed_mask(layout[0], layout[2]).T, 0.0, -1e30).astype(jnp.float32)
            for layout in layouts
        ]
    )
    scale_one = rms_scale(inputs)

    scale_one = tick(scale_one, [], [out_rows, down_rows])
    scale_one = tick(scale_one, [out_rows, down_rows], [out_rows])
    scale_one = tick(scale_one, [out_rows], [])
    gain_first_f = first_set[:, 3 * model_width].astype(jnp.float32)[None, :]
    gain_second_f = first_set[:, 3 * model_width + 1].astype(jnp.float32)[None, :]
    normed = (inputs * scale_one * gain_first_f).astype(jnp.bfloat16)
    normed = tick(normed, [], [out_rows, down_rows])
    query_rot, key_rot, value_mix, context, lse = attend(
        normed, first_set, first_values, bias, cosine, sine, head_size, width
    )
    context = tick(context, [out_rows, down_rows], [out_rows, down_rows])
    while out_rows.steps:
        context = tick(context, [out_rows], [out_rows])
    out_w = out_rows.current
    hidden = inputs + forward_dot(context, out_w)
    scale_two = rms_scale(hidden)
    normed_two = (hidden * scale_two * gain_second_f).astype(jnp.bfloat16)
    gate_w = second_set[:, :hidden_width]
    up_w = second_set[:, hidden_width:]
    while down_rows.steps:
        normed_two = tick(normed_two, [down_rows], [down_rows])
    down_w = down_rows.current
    grad_y = cotangent.astype(jnp.float32) * valid.astype(jnp.float32)[:, None]
    grad_y_low = grad_y.astype(jnp.bfloat16)
    grad_product = contract_last(grad_y_low, down_w)
    core_bit = fsdp_size.bit_length() - 1
    normed_t, context_t, two_t = [
        jnp.concatenate(split_columns(matrix, core_bit, place, device_count), axis=1).T
        for matrix in (normed, context, normed_two)
    ]
    normed_two, grad_product, normed_t, context_t, two_t = lax.optimization_barrier(
        (normed_two, grad_product, normed_t, context_t, two_t)
    )
    product, grad_gate_low, grad_upward, *feed_parts = feed(
        normed_two, two_t, grad_y_low, grad_product, second_set
    )
    gate_parts, up_parts = [
        [part[None] for part in feed_parts[start : start + 2]] for start in (0, 2)
    ]
    gate = exchange(None, plans["low_first"], first=gate_parts)
    up = exchange(None, plans["high_first"], first=up_parts)
    down = exchange(feed_parts[4][None], plans["high_first"])
    grad_upward, grad_gate_low = tick((grad_upward, grad_gate_low), [], [gate, up, down])
    grad_normed_two = contract_last(grad_gate_low, gate_w) + contract_last(grad_upward, up_w)
    grad_normed_two = tick(grad_normed_two, [gate, up, down], [gate, up])
    inner_two = grad_normed_two * gain_second_f
    grad_hidden = (
        grad_y
        + scale_two * inner_two
        - hidden * scale_two**3 * jnp.mean(inner_two * hidden, axis=-1, keepdims=True)
    )
    grad_hidden_low = grad_hidden.astype(jnp.bfloat16)
    grad_context = contract_last(grad_hidden_low, out_w).astype(jnp.bfloat16)
    def attend_back_half(half, grad_context, first, outs):
        return attend_back(
            query_rot,
            key_rot,
            value_mix,
            grad_context,
            lse,
            bias,
            cosine,
            sine,
            normed_t,
            *outs,
            head_size,
            width,
            half * half_steps,
            half_steps,
            first,
        )

    low_one, first_part, *parts_one = attend_back_half(
        0, grad_context, None, (context_t, grad_hidden_low)
    )
    one = exchange(None, plans["low_first"], first=parts_one)
    grad_context, product = tick((grad_context, product), [gate, up], [gate, up, one])
    out_tokens = (hidden + forward_dot(product, down_w)).astype(jnp.bfloat16)
    grad_context, out_tokens = tick(
        (grad_context, out_tokens), [gate, up, one], [down, one, gate, up]
    )
    low_two, grad_first, *parts_two = attend_back_half(1, grad_context, first_part, (None, None))
    two = exchange(None, plans["short"], first=parts_two)
    low_two = tick(low_two, [down, one, gate, up], [two, down, one, gate, up])
    grad_tokens = finish(
        low_one, low_two, first_set, grad_hidden, tokens, scale_one, gain_first_f
    )
    grad_tokens = tick(grad_tokens, [two, down, one, gate, up], [two, down, one])
    pending = [two, down, one, gate, up]
    while any(item.steps for item in pending):
        grad_tokens = tick(grad_tokens, pending, pending)
    projection_sums = [
        jnp.concatenate([one.current[index], two.current[index]], axis=1) for index in range(3)
    ]
    grad_out_sum = jnp.concatenate([one.current[3], one.current[4]], axis=1)
    grad_gate_sum = gate.current[0]
    grad_up_sum = up.current[0]
    grad_down_sum = down.current[0]

    def gain_grad(gain, sums, weights):
        total = sum(
            jnp.sum(grads * weight.astype(jnp.float32), axis=1)
            for grads, weight in zip(sums, weights)
        )
        return total / gain.astype(jnp.float32)

    return (
        out_tokens,
        grad_tokens,
        grad_first,
        *projection_sums,
        grad_out_sum,
        grad_gate_sum,
        grad_up_sum,
        grad_down_sum,
        gain_grad(gain_one, projection_sums, projections),
        gain_grad(gain_two, (grad_gate_sum, grad_up_sum), (w_gate, w_up)),
    )


def solution(mesh):
    rows = P(AXES, None)
    ends = P(AXES)
    return jax.shard_map(
        partial(shards, mesh.shape["dp"], mesh.shape["fsdp"]),
        mesh=mesh,
        in_specs=(rows,) * 11 + (ends,) * 2,
        out_specs=(rows,) * 10 + (ends,) * 2,
        check_vma=False,
    )
```

```python
import math
from functools import partial

import jax
import jax.numpy as jnp
from jax import lax
from jax.experimental import pallas as pl
from jax.experimental.pallas import tpu as pltpu
from jax.sharding import PartitionSpec as P

HEADS = 16


EPSILON = 1e-06


def forward_dot(left, right):
    return jnp.dot(left, right, preferred_element_type=jnp.float32)


def contract_last(left, right):
    return lax.dot_general(
        left, right, (((1,), (1,)), ((), ())), preferred_element_type=jnp.float32
    )


def contract_first(left, right):
    return lax.dot_general(
        left, right, (((0,), (0,)), ((), ())), preferred_element_type=jnp.float32
    )


def bucket_layout(lengths_row, slot_count):
    seq_ends = jnp.cumsum(lengths_row)
    slot_places = jnp.arange(slot_count, dtype=jnp.int32)
    ended_mask = seq_ends[None, :] <= slot_places[:, None]
    segment = jnp.sum(ended_mask.astype(jnp.int32), axis=1)
    before_total = jnp.sum(jnp.where(ended_mask, lengths_row[None, :], 0), axis=1)
    return (segment, slot_places - before_total, slot_places < seq_ends[-1])


def rope_tables(position, head_size):
    half_size = head_size // 2
    frequency = jnp.exp(
        jnp.arange(half_size, dtype=jnp.float32) * (-2.0 * math.log(10000.0) / head_size)
    )
    angles = position.astype(jnp.float32)[:, None] * frequency[None, :]
    return (jnp.cos(angles), jnp.sin(angles))


def allowed_mask(segment, valid):
    slot_places = jnp.arange(segment.shape[0])
    earlier = slot_places[None, :] < slot_places[:, None]
    same_seq = segment[:, None] == segment[None, :]
    diagonal = slot_places[None, :] == slot_places[:, None]
    return diagonal | same_seq & earlier & valid[:, None]


def rms_scale(matrix):
    return lax.rsqrt(jnp.mean(matrix * matrix, axis=-1, keepdims=True) + EPSILON)


PAIR = 128


def swap_halves(matrix, half_size):
    lane = lax.broadcasted_iota(jnp.int32, matrix.shape, 1)
    first = lane % (2 * half_size) < half_size
    width = matrix.shape[1]
    return jnp.where(
        first, pltpu.roll(matrix, width - half_size, 1), pltpu.roll(matrix, half_size, 1)
    )


def head_part(matrix, head, head_size):
    lane = lax.broadcasted_iota(jnp.int32, matrix.shape, 1)
    return jnp.where(lane // head_size == head, matrix, jnp.zeros_like(matrix))


def attend_kernel(
    slot_count,
    head_size,
    normed_ref,
    wq_ref,
    wk_ref,
    wv_ref,
    first_ref,
    bias_ref,
    cos_ref,
    sin_ref,
    q_ref,
    k_ref,
    v_ref,
    ctx_ref,
    lse_ref,
):
    half_size = head_size // 2
    score_scale = head_size ** (-0.5)
    width = q_ref.shape[1]
    bucket_count = bias_ref.shape[0]
    query_rows = slot_count // 2
    normed = normed_ref[...]
    cosine = cos_ref[...]
    sine = sin_ref[...]
    for raw_ref, w_ref in ((q_ref, wq_ref), (k_ref, wk_ref)):
        raw = forward_dot(normed, w_ref[...])
        for low in range(0, width, PAIR):
            part = raw[:, low : low + PAIR]
            raw_ref[:, low : low + PAIR] = (
                part * cosine + swap_halves(part, half_size) * sine
            ).astype(jnp.bfloat16)
    v_ref[...] = (
        0.5 * forward_dot(normed, wv_ref[...]) + 0.5 * first_ref[...].astype(jnp.float32)
    ).astype(jnp.bfloat16)
    for bucket in range(bucket_count):
        base = bucket * slot_count
        for low in range(0, width, PAIR):
            keys = k_ref[base : base + slot_count, low : low + PAIR]
            queries = q_ref[base : base + slot_count, low : low + PAIR] * score_scale
            values_t = v_ref[base : base + slot_count, low : low + PAIR].T
            for start in range(0, slot_count, query_rows):
                end = start + query_rows
                parts = []
                for head in range(PAIR // head_size):
                    key_head = head_part(keys[:end], head, head_size)
                    scores = (
                        contract_last(key_head, queries[start:end])
                        + bias_ref[bucket, :end, start:end]
                    )
                    top = jnp.max(scores, axis=0, keepdims=True)
                    weights = jnp.exp(scores - top)
                    mass = jnp.sum(weights, axis=0, keepdims=True)
                    row = (low // head_size) + head
                    lse_ref[bucket, 0, row : row + 1, start:end] = top + jnp.log(mass)
                    mixed = forward_dot(
                        values_t[head * head_size : (head + 1) * head_size, :end],
                        weights.astype(jnp.bfloat16),
                    )
                    parts.append(mixed * (1.0 / mass))
                ctx_ref[base + start : base + end, low : low + PAIR] = (
                    jnp.concatenate(parts, axis=0).T.astype(jnp.bfloat16)
                )


def attend(normed, weights, first_values, bias, cosine, sine, head_size, width):
    token_count, model_width = normed.shape
    bucket_count, slot_count = bias.shape[:2]
    steps = model_width // width
    whole = lambda step: (0, 0)
    block = pl.BlockSpec((token_count, width), lambda step: (0, step))
    heads = width // head_size
    table = pl.BlockSpec((token_count, PAIR), whole)
    low_shape = jax.ShapeDtypeStruct((token_count, steps * width), jnp.bfloat16)
    return pl.pallas_call(
        partial(attend_kernel, slot_count, head_size),
        grid=(steps,),
        in_specs=[
            pl.BlockSpec((token_count, model_width), whole),
            pl.BlockSpec((model_width, width), lambda step: (0, step)),
            pl.BlockSpec((model_width, width), lambda step: (0, steps + step)),
            pl.BlockSpec((model_width, width), lambda step: (0, 2 * steps + step)),
            block,
            pl.BlockSpec((bucket_count, slot_count, slot_count), lambda step: (0, 0, 0)),
            table,
            table,
        ],
        out_specs=[
            block,
            block,
            block,
            block,
            pl.BlockSpec((bucket_count, 1, heads, slot_count), lambda step: (0, step, 0, 0)),
        ],
        out_shape=[low_shape] * 4
        + [jax.ShapeDtypeStruct((bucket_count, steps, heads, slot_count), jnp.float32)],
        compiler_params=pltpu.CompilerParams(vmem_limit_bytes=56 << 20),
        name="attend",
    )(normed, weights, weights, weights, first_values, bias, cosine, sine)


def attend_back_kernel(
    slot_count,
    head_size,
    q_ref,
    k_ref,
    v_ref,
    grad_ref,
    lse_ref,
    bias_ref,
    cos_ref,
    sin_ref,
    *rest,
):
    normed_t_ref = rest[0]
    grads_ref, first_ref, kept_ref, sent_ref, dk_ref, dv_ref = rest[-6:]
    half_size = head_size // 2
    score_scale = head_size ** (-0.5)
    width = q_ref.shape[1]
    bucket_count = bias_ref.shape[0]
    query_rows = slot_count // 2
    head_count = PAIR // head_size
    for bucket in range(bucket_count):
        base = bucket * slot_count
        cosine = cos_ref[base : base + slot_count]
        sine = sin_ref[base : base + slot_count]
        for low in range(0, width, PAIR):
            keys = k_ref[base : base + slot_count, low : low + PAIR]
            values = v_ref[base : base + slot_count, low : low + PAIR]
            queries = q_ref[base : base + slot_count, low : low + PAIR] * score_scale
            grads = grad_ref[base : base + slot_count, low : low + PAIR]
            keys_t = keys.T
            query_parts = []
            for start in range(0, slot_count, query_rows):
                end = start + query_rows
                parts = []
                for head in range(head_count):
                    row = (low // head_size) + head
                    scores = contract_last(
                        head_part(keys[:end], head, head_size), queries[start:end]
                    )
                    probs = jnp.exp(
                        scores
                        + bias_ref[bucket, :end, start:end]
                        - lse_ref[bucket, 0, row : row + 1, start:end]
                    )
                    grad_probs = contract_last(
                        head_part(values[:end], head, head_size), grads[start:end]
                    )
                    weighted = probs * grad_probs
                    grad_scores = (
                        weighted - probs * jnp.sum(weighted, axis=0, keepdims=True)
                    ).astype(jnp.bfloat16)
                    dv = forward_dot(probs.astype(jnp.bfloat16), grads[start:end])
                    dk = forward_dot(grad_scores, queries[start:end])
                    if start == 0:
                        dv_ref[head, :end] = dv
                        dk_ref[head, :end] = dk
                    else:
                        dv_ref[head, :start] += dv[:start]
                        dk_ref[head, :start] += dk[:start]
                        dv_ref[head, start:end] = dv[start:]
                        dk_ref[head, start:end] = dk[start:]
                    parts.append(
                        forward_dot(
                            keys_t[head * head_size : (head + 1) * head_size, :end], grad_scores
                        )
                    )
                query_parts.append((jnp.concatenate(parts, axis=0) * score_scale).T)
            lane = lax.broadcasted_iota(jnp.int32, (slot_count, PAIR), 1)
            dv = dv_ref[0]
            dk = dk_ref[0]
            for head in range(1, head_count):
                here = lane // head_size == head
                dv = jnp.where(here, dv_ref[head], dv)
                dk = jnp.where(here, dk_ref[head], dk)
            dq = jnp.concatenate(query_parts, axis=0)
            rows = slice(base, base + slot_count)
            for index, part in enumerate((dq, dk)):
                grads_ref[index, rows, low : low + PAIR] = (
                    part * cosine - swap_halves(part, half_size) * sine
                ).astype(jnp.bfloat16)
            first_ref[rows, low : low + PAIR] = 0.5 * dv
            grads_ref[2, rows, low : low + PAIR] = (0.5 * dv).astype(jnp.bfloat16)
    products = [(normed_t_ref, grads_ref.at[index]) for index in range(3)]
    if kept_ref.shape[0] > 3:
        products += [(rest[1], rest[2]), (rest[1], rest[3])]
    half = kept_ref.shape[1]
    for index, (left_ref, right_ref) in enumerate(products):
        right = right_ref[...]
        kept_ref[index] = forward_dot(left_ref[:half], right).astype(jnp.bfloat16)
        sent_ref[index] = forward_dot(left_ref[half:], right).astype(jnp.bfloat16)


def attend_back(
    queries,
    keys,
    values,
    grads,
    lse,
    bias,
    cosine,
    sine,
    normed_t,
    context_t,
    grad_hidden_low,
    head_size,
    width,
    first_step,
    steps,
    first,
):
    token_count, model_width = queries.shape
    bucket_count, slot_count = bias.shape[:2]
    heads = width // head_size
    block = pl.BlockSpec((token_count, width), lambda step: (0, first_step + step))
    table = pl.BlockSpec((token_count, PAIR), lambda step: (0, 0))
    lead = 3 if context_t is None else 5
    out_args = [] if context_t is None else [context_t, grad_hidden_low, grad_hidden_low]
    shared = [] if first is None else [first]
    return pl.pallas_call(
        partial(attend_back_kernel, slot_count, head_size),
        grid=(steps,),
        in_specs=[
            block,
            block,
            block,
            block,
            pl.BlockSpec(
                (bucket_count, 1, heads, slot_count), lambda step: (0, first_step + step, 0, 0)
            ),
            pl.BlockSpec((bucket_count, slot_count, slot_count), lambda step: (0, 0, 0)),
            table,
            table,
            pl.BlockSpec((model_width, token_count), lambda step: (0, 0)),
            pl.BlockSpec((model_width, token_count), lambda step: (0, 0)),
            pl.BlockSpec((token_count, width), lambda step: (0, step)),
            pl.BlockSpec((token_count, width), lambda step: (0, steps + step)),
        ][: 9 + len(out_args)]
        + [pl.BlockSpec(memory_space=pl.ANY)] * len(shared),
        out_specs=[
            pl.BlockSpec((3, token_count, width), lambda step: (0, 0, step)),
            block,
        ]
        + [pl.BlockSpec((lead, model_width // 2, width), lambda step: (0, 0, step))] * 2,
        out_shape=[
            jax.ShapeDtypeStruct((3, token_count, steps * width), jnp.bfloat16),
            jax.ShapeDtypeStruct((token_count, model_width), jnp.float32),
        ]
        + [jax.ShapeDtypeStruct((lead, model_width // 2, steps * width), jnp.bfloat16)] * 2,
        scratch_shapes=[
            pltpu.VMEM((PAIR // head_size, slot_count, PAIR), jnp.float32),
            pltpu.VMEM((PAIR // head_size, slot_count, PAIR), jnp.float32),
        ],
        input_output_aliases={9 + len(out_args): 1} if shared else {},
        compiler_params=pltpu.CompilerParams(vmem_limit_bytes=56 << 20),
        cost_estimate=pl.CostEstimate(flops=1, transcendentals=0, bytes_accessed=1),
        name="attend_back",
    )(queries, keys, values, grads, lse, bias, cosine, sine, normed_t, *out_args, *shared)


def feed_kernel(
    normed_ref,
    normed_t_ref,
    grad_y_ref,
    grad_product_ref,
    gate_ref,
    up_ref,
    product_ref,
    grad_gate_ref,
    grad_up_ref,
    gate_kept_ref,
    gate_sent_ref,
    up_kept_ref,
    up_sent_ref,
    down_ref,
):
    gate_values = forward_dot(normed_ref[...], gate_ref[...])
    upward = forward_dot(normed_ref[...], up_ref[...])
    grad_product = grad_product_ref[...]
    sigmoid_gate = jax.nn.sigmoid(gate_values)
    silu_gate = gate_values * sigmoid_gate
    product = (silu_gate * upward).astype(jnp.bfloat16)
    product_ref[...] = product
    grad_up_ref[...] = (grad_product * silu_gate).astype(jnp.bfloat16)
    grad_gate_ref[...] = (
        grad_product * upward * sigmoid_gate * (1.0 + gate_values * (1.0 - sigmoid_gate))
    ).astype(jnp.bfloat16)
    half = gate_kept_ref.shape[0]
    for grads_ref, kept_ref, sent_ref in (
        (grad_gate_ref, gate_kept_ref, gate_sent_ref),
        (grad_up_ref, up_kept_ref, up_sent_ref),
    ):
        grads = grads_ref[...]
        kept_ref[...] = forward_dot(normed_t_ref[:half], grads).astype(jnp.bfloat16)
        sent_ref[...] = forward_dot(normed_t_ref[half:], grads).astype(jnp.bfloat16)
    down_ref[...] = forward_dot(product.T, grad_y_ref[...]).astype(jnp.bfloat16)


def feed(normed, normed_t, grad_y, grad_product, weights):
    token_count, model_width = normed.shape
    hidden_width = grad_product.shape[1]
    width = 256
    steps = hidden_width // width
    whole = lambda step: (0, 0)
    wide = pl.BlockSpec((token_count, width), lambda step: (0, step))
    half = pl.BlockSpec((model_width // 2, width), lambda step: (0, step))
    wide_shape = jax.ShapeDtypeStruct((token_count, hidden_width), jnp.bfloat16)
    half_shape = jax.ShapeDtypeStruct((model_width // 2, hidden_width), jnp.bfloat16)
    return pl.pallas_call(
        feed_kernel,
        grid=(steps,),
        in_specs=[
            pl.BlockSpec((token_count, model_width), whole),
            pl.BlockSpec((model_width, token_count), whole),
            pl.BlockSpec((token_count, model_width), whole),
            wide,
            pl.BlockSpec((model_width, width), lambda step: (0, step)),
            pl.BlockSpec((model_width, width), lambda step: (0, steps + step)),
        ],
        out_specs=[wide] * 3
        + [half] * 4
        + [pl.BlockSpec((width, model_width), lambda step: (step, 0))],
        out_shape=[wide_shape] * 3
        + [half_shape] * 4
        + [jax.ShapeDtypeStruct((hidden_width, model_width), jnp.bfloat16)],
        compiler_params=pltpu.CompilerParams(vmem_limit_bytes=56 << 20),
        cost_estimate=pl.CostEstimate(flops=1, transcendentals=0, bytes_accessed=1),
        name="feed",
    )(normed, normed_t, grad_y, grad_product, weights, weights)


def finish_kernel(
    low_one_ref,
    low_two_ref,
    wq_ref,
    wk_ref,
    wv_ref,
    hidden_ref,
    x_ref,
    scale_ref,
    gain_ref,
    out_ref,
):
    half = low_one_ref.shape[2]
    total = None
    for index, w_ref in enumerate((wq_ref, wk_ref, wv_ref)):
        for low_ref, start in ((low_one_ref, 0), (low_two_ref, half)):
            part = contract_last(low_ref[index], w_ref[:, start : start + half])
            total = part if total is None else total + part
    inner = total * gain_ref[...]
    inputs = x_ref[...].astype(jnp.float32)
    scale = scale_ref[...]
    mean = jnp.mean(inner * inputs, axis=-1, keepdims=True)
    out_ref[...] = hidden_ref[...] + scale * inner - inputs * scale**3 * mean


def finish(low_one, low_two, weights, grad_hidden, inputs, scale, gain):
    token_count, model_width = inputs.shape
    rows = token_count // 4
    row_block = pl.BlockSpec((rows, model_width), lambda step: (step, 0))
    low_block = pl.BlockSpec((3, rows, model_width // 2), lambda step: (0, step, 0))
    weight_blocks = [
        pl.BlockSpec((model_width, model_width), lambda step, index=index: (0, index))
        for index in range(3)
    ]
    return pl.pallas_call(
        finish_kernel,
        grid=(4,),
        in_specs=[low_block, low_block]
        + weight_blocks
        + [
            row_block,
            row_block,
            pl.BlockSpec((rows, 1), lambda step: (step, 0)),
            pl.BlockSpec((1, model_width), lambda step: (0, 0)),
        ],
        out_specs=row_block,
        out_shape=jax.ShapeDtypeStruct((token_count, model_width), jnp.float32),
        compiler_params=pltpu.CompilerParams(vmem_limit_bytes=56 << 20),
        cost_estimate=pl.CostEstimate(flops=1, transcendentals=0, bytes_accessed=1),
        name="finish",
    )(low_one, low_two, weights, weights, weights, grad_hidden, inputs, scale, gain)


AXES = ("dp", "fsdp")


def flip(value, mask, device_count):
    pairs = [(place, place ^ mask) for place in range(device_count)]
    return lax.ppermute(value, AXES, pairs)


def masks_of(bits):
    masks = [0]
    for bit in bits:
        masks += [mask | 1 << bit for mask in masks]
    return masks


class Exchange:
    def __init__(self, partial_sum, steps, place, device_count, first=None):
        self.current = partial_sum
        self.first = first
        self.steps = [list(step) for step in steps]
        self.left = sorted([bit for step in steps for bit in step], reverse=True)
        self.place = place
        self.device_count = device_count
        self.got = None

    def part(self, mask):
        value = self.current
        left = list(self.left)
        for bit in self.steps[0]:
            lead, row_count, width = value.shape
            high = 1 << left.index(bit)
            view = value.reshape(lead, high, 2, row_count // (2 * high), width)
            chosen = ((self.place ^ mask) >> bit) & 1
            value = lax.dynamic_index_in_dim(view, chosen, 2, keepdims=False)
            value = value.reshape(lead, row_count // 2, width)
            left.remove(bit)
        return value

    def outgoing(self):
        if self.first is not None:
            self.kept, sent = self.first
            self.first = None
            return [sent]
        masks = masks_of(self.steps[0])
        self.kept = self.part(0)
        return [self.part(mask) for mask in masks[1:]]

    def launch(self, sent):
        masks = masks_of(self.steps[0])[1:]
        self.got = [flip(value, mask, self.device_count) for value, mask in zip(sent, masks)]

    def settle(self, got):
        total = self.kept.astype(jnp.float32)
        for value in got:
            total = total + value.astype(jnp.float32)
        for bit in self.steps.pop(0):
            self.left.remove(bit)
        self.current = total.astype(jnp.bfloat16) if self.steps else total


class Gather:
    def __init__(self, rows, steps, place, device_count):
        self.current = rows
        self.steps = [list(step) for step in steps]
        self.have = []
        self.place = place
        self.device_count = device_count
        self.got = None

    def outgoing(self):
        return [self.current]

    def launch(self, sent):
        masks = masks_of(self.steps[0])[1:]
        self.got = [flip(sent[0], mask, self.device_count) for mask in masks]

    def settle(self, got):
        pieces = [self.current] + list(got)
        for bit in self.steps.pop(0):
            row_count, width = pieces[0].shape
            high = 1 << len([other for other in self.have if other > bit])
            shape = (high, 1, row_count // high, width)
            side = lax.broadcasted_iota(jnp.int32, (1, 2, 1, 1), 1)
            mine = side == ((self.place >> bit) & 1)
            pieces = [
                jnp.where(mine, near.reshape(shape), far.reshape(shape)).reshape(
                    2 * row_count, width
                )
                for near, far in zip(pieces[0::2], pieces[1::2])
            ]
            self.have.append(bit)
        self.current = pieces[0]


def split_columns(matrix, bit, place, device_count):
    row_count, column_count = matrix.shape
    low = (column_count // device_count) << bit
    mine = (place >> bit) & 1
    return [
        jnp.concatenate(
            [
                lax.dynamic_slice(matrix, (0, start + side * low), (row_count, low))
                for start in range(0, column_count, 2 * low)
            ],
            axis=1,
        )
        for side in (mine, 1 - mine)
    ]


def tick(chain, settled, launched):
    settled = [item for item in settled if item.got is not None]
    if settled:
        chain, gots = lax.optimization_barrier((chain, [item.got for item in settled]))
        for item, got in zip(settled, gots):
            item.settle(got)
            item.got = None
    launched = [item for item in launched if item.steps and item.got is None]
    if launched:
        chain, sents = lax.optimization_barrier((chain, [item.outgoing() for item in launched]))
        for item, sent in zip(launched, sents):
            item.launch(sent)
    return chain


def step_plans(dp_size, fsdp_size):
    bit_count = (dp_size * fsdp_size).bit_length() - 1
    core_bit = fsdp_size.bit_length() - 1
    high = list(range(core_bit + 1, bit_count))
    rest = list(range(1, core_bit))
    pairs = [rest[index : index + 2] for index in range(0, len(rest), 2)]
    core = [core_bit]
    singles = [[bit] for bit in rest]
    return {
        "high_first": [core, high, [0]] + singles,
        "low_first": [core, [0], high] + singles,
        "short": [core, high + [0]] + pairs,
        "gather": pairs[::-1] + [[0] + high, core],
    }


def shards(
    dp_size,
    fsdp_size,
    tokens,
    first_values,
    cotangent,
    lengths,
    w_query,
    w_key,
    w_value,
    w_out,
    w_gate,
    w_up,
    w_down,
    gain_one,
    gain_two,
):
    device_count = dp_size * fsdp_size
    place = lax.axis_index("dp") * fsdp_size + lax.axis_index("fsdp")
    plans = step_plans(dp_size, fsdp_size)
    micro_count = lengths.shape[0]
    token_count, model_width = tokens.shape
    slot_count = token_count // micro_count
    head_size = model_width // HEADS
    hidden_width = w_gate.shape[1]
    width = 4 * head_size
    half_width = model_width // 2
    half_steps = half_width // width
    exchange = partial(Exchange, place=place, device_count=device_count)

    gain_columns = jnp.pad(jnp.stack([gain_one, gain_two], axis=1), ((0, 0), (0, 126)))
    gather = partial(Gather, place=place, device_count=device_count)
    projections = (w_query, w_key, w_value)
    first_set = lax.all_gather(
        jnp.concatenate([*projections, gain_columns], axis=1), AXES, axis=0, tiled=True
    )
    second_set = lax.all_gather(
        jnp.concatenate([w_gate, w_up], axis=1), AXES, axis=0, tiled=True
    )
    out_rows = gather(w_out, plans["gather"])
    down_rows = gather(w_down, plans["gather"])

    inputs = tokens.astype(jnp.float32)
    layouts = [bucket_layout(lengths[index], slot_count) for index in range(micro_count)]
    position = jnp.concatenate([layout[1] for layout in layouts])
    valid = jnp.concatenate([layout[2] for layout in layouts])
    cosine, sine = rope_tables(position, head_size)
    cosine = jnp.tile(cosine, (1, 2 * PAIR // head_size))
    sine = jnp.tile(jnp.concatenate([-sine, sine], axis=1), (1, PAIR // head_size))
    bias = jnp.stack(
        [
            jnp.where(allowed_mask(layout[0], layout[2]).T, 0.0, -1e30).astype(jnp.float32)
            for layout in layouts
        ]
    )
    scale_one = rms_scale(inputs)

    scale_one, cosine, sine, bias = tick(
        (scale_one, cosine, sine, bias), [], [out_rows, down_rows]
    )
    scale_one, cosine, sine, bias = tick(
        (scale_one, cosine, sine, bias), [out_rows, down_rows], [out_rows]
    )
    scale_one = tick(scale_one, [out_rows], [])
    gain_first_f = first_set[:, 3 * model_width].astype(jnp.float32)[None, :]
    gain_second_f = first_set[:, 3 * model_width + 1].astype(jnp.float32)[None, :]
    normed = (inputs * scale_one * gain_first_f).astype(jnp.bfloat16)
    normed = tick(normed, [], [out_rows, down_rows])
    query_rot, key_rot, value_mix, context, lse = attend(
        normed, first_set, first_values, bias, cosine, sine, head_size, width
    )
    context = tick(context, [out_rows, down_rows], [out_rows, down_rows])
    while out_rows.steps:
        context = tick(context, [out_rows], [out_rows])
    out_w = out_rows.current
    hidden = inputs + forward_dot(context, out_w)
    scale_two = rms_scale(hidden)
    normed_two = (hidden * scale_two * gain_second_f).astype(jnp.bfloat16)
    gate_w = second_set[:, :hidden_width]
    up_w = second_set[:, hidden_width:]
    while down_rows.steps:
        normed_two = tick(normed_two, [down_rows], [down_rows])
    down_w = down_rows.current
    grad_y = cotangent.astype(jnp.float32) * valid.astype(jnp.float32)[:, None]
    grad_y_low = grad_y.astype(jnp.bfloat16)
    grad_product = contract_last(grad_y_low, down_w)
    core_bit = fsdp_size.bit_length() - 1
    normed_t, context_t, two_t = [
        jnp.concatenate(split_columns(matrix, core_bit, place, device_count), axis=1).T
        for matrix in (normed, context, normed_two)
    ]
    normed_two, grad_product, normed_t, context_t, two_t = lax.optimization_barrier(
        (normed_two, grad_product, normed_t, context_t, two_t)
    )
    product, grad_gate_low, grad_upward, *feed_parts = feed(
        normed_two, two_t, grad_y_low, grad_product, second_set
    )
    gate_parts, up_parts = [
        [part[None] for part in feed_parts[start : start + 2]] for start in (0, 2)
    ]
    gate = exchange(None, plans["low_first"], first=gate_parts)
    up = exchange(None, plans["high_first"], first=up_parts)
    down = exchange(feed_parts[4][None], plans["high_first"])
    grad_upward, grad_gate_low = tick((grad_upward, grad_gate_low), [], [gate, up, down])
    grad_normed_two = contract_last(grad_gate_low, gate_w) + contract_last(grad_upward, up_w)
    grad_normed_two = tick(grad_normed_two, [gate, up, down], [gate, up])
    inner_two = grad_normed_two * gain_second_f
    grad_hidden = (
        grad_y
        + scale_two * inner_two
        - hidden * scale_two**3 * jnp.mean(inner_two * hidden, axis=-1, keepdims=True)
    )
    grad_hidden_low = grad_hidden.astype(jnp.bfloat16)
    grad_context = contract_last(grad_hidden_low, out_w).astype(jnp.bfloat16)
    def attend_back_half(half, grad_context, first, outs):
        return attend_back(
            query_rot,
            key_rot,
            value_mix,
            grad_context,
            lse,
            bias,
            cosine,
            sine,
            normed_t,
            *outs,
            head_size,
            width,
            half * half_steps,
            half_steps,
            first,
        )

    low_one, first_part, *parts_one = attend_back_half(
        0, grad_context, None, (context_t, grad_hidden_low)
    )
    one = exchange(None, plans["low_first"], first=parts_one)
    grad_context, product = tick((grad_context, product), [gate, up], [gate, up, one])
    out_tokens = (hidden + forward_dot(product, down_w)).astype(jnp.bfloat16)
    grad_context, out_tokens = tick(
        (grad_context, out_tokens), [gate, up, one], [down, one, gate, up]
    )
    low_two, grad_first, *parts_two = attend_back_half(1, grad_context, first_part, (None, None))
    two = exchange(None, plans["short"], first=parts_two)
    low_two = tick(low_two, [down, one, gate, up], [two, down, one, gate, up])
    grad_tokens = finish(
        low_one, low_two, first_set, grad_hidden, tokens, scale_one, gain_first_f
    )
    grad_tokens = tick(grad_tokens, [two, down, one, gate, up], [two, down, one])
    pending = [two, down, one, gate, up]
    while any(item.steps for item in pending):
        grad_tokens = tick(grad_tokens, pending, pending)
    projection_sums = [
        jnp.concatenate([one.current[index], two.current[index]], axis=1) for index in range(3)
    ]
    grad_out_sum = jnp.concatenate([one.current[3], one.current[4]], axis=1)
    grad_gate_sum = gate.current[0]
    grad_up_sum = up.current[0]
    grad_down_sum = down.current[0]

    def gain_grad(gain, sums, weights):
        total = sum(
            jnp.sum(grads * weight.astype(jnp.float32), axis=1)
            for grads, weight in zip(sums, weights)
        )
        return total / gain.astype(jnp.float32)

    return (
        out_tokens,
        grad_tokens,
        grad_first,
        *projection_sums,
        grad_out_sum,
        grad_gate_sum,
        grad_up_sum,
        grad_down_sum,
        gain_grad(gain_one, projection_sums, projections),
        gain_grad(gain_two, (grad_gate_sum, grad_up_sum), (w_gate, w_up)),
    )


def solution(mesh):
    rows = P(AXES, None)
    ends = P(AXES)
    return jax.shard_map(
        partial(shards, mesh.shape["dp"], mesh.shape["fsdp"]),
        mesh=mesh,
        in_specs=(rows,) * 11 + (ends,) * 2,
        out_specs=(rows,) * 10 + (ends,) * 2,
        check_vma=False,
    )
```

```python
import math
from functools import partial

import jax
import jax.numpy as jnp
from jax import lax
from jax.experimental import pallas as pl
from jax.experimental.pallas import tpu as pltpu
from jax.sharding import PartitionSpec as P

HEADS = 16


EPSILON = 1e-06


def forward_dot(left, right):
    return jnp.dot(left, right, preferred_element_type=jnp.float32)


def contract_last(left, right):
    return lax.dot_general(
        left, right, (((1,), (1,)), ((), ())), preferred_element_type=jnp.float32
    )


def contract_first(left, right):
    return lax.dot_general(
        left, right, (((0,), (0,)), ((), ())), preferred_element_type=jnp.float32
    )


def bucket_layout(lengths_row, slot_count):
    seq_ends = jnp.cumsum(lengths_row)
    slot_places = jnp.arange(slot_count, dtype=jnp.int32)
    ended_mask = seq_ends[None, :] <= slot_places[:, None]
    segment = jnp.sum(ended_mask.astype(jnp.int32), axis=1)
    before_total = jnp.sum(jnp.where(ended_mask, lengths_row[None, :], 0), axis=1)
    return (segment, slot_places - before_total, slot_places < seq_ends[-1])


def rope_tables(position, head_size):
    half_size = head_size // 2
    frequency = jnp.exp(
        jnp.arange(half_size, dtype=jnp.float32) * (-2.0 * math.log(10000.0) / head_size)
    )
    angles = position.astype(jnp.float32)[:, None] * frequency[None, :]
    return (jnp.cos(angles), jnp.sin(angles))


def allowed_mask(segment, valid):
    slot_places = jnp.arange(segment.shape[0])
    earlier = slot_places[None, :] < slot_places[:, None]
    same_seq = segment[:, None] == segment[None, :]
    diagonal = slot_places[None, :] == slot_places[:, None]
    return diagonal | same_seq & earlier & valid[:, None]


def rms_scale(matrix):
    return lax.rsqrt(jnp.mean(matrix * matrix, axis=-1, keepdims=True) + EPSILON)


PAIR = 128


def swap_halves(matrix, half_size):
    lane = lax.broadcasted_iota(jnp.int32, matrix.shape, 1)
    first = lane % (2 * half_size) < half_size
    width = matrix.shape[1]
    return jnp.where(
        first, pltpu.roll(matrix, width - half_size, 1), pltpu.roll(matrix, half_size, 1)
    )


def head_part(matrix, head, head_size):
    lane = lax.broadcasted_iota(jnp.int32, matrix.shape, 1)
    return jnp.where(lane // head_size == head, matrix, jnp.zeros_like(matrix))


def attend_kernel(
    slot_count,
    head_size,
    normed_ref,
    wq_ref,
    wk_ref,
    wv_ref,
    first_ref,
    bias_ref,
    cos_ref,
    sin_ref,
    q_ref,
    k_ref,
    v_ref,
    ctx_ref,
    lse_ref,
):
    half_size = head_size // 2
    score_scale = head_size ** (-0.5)
    width = q_ref.shape[1]
    bucket_count = bias_ref.shape[0]
    query_rows = slot_count // 2
    normed = normed_ref[...]
    cosine = cos_ref[...]
    sine = sin_ref[...]
    for raw_ref, w_ref in ((q_ref, wq_ref), (k_ref, wk_ref)):
        raw = forward_dot(normed, w_ref[...])
        for low in range(0, width, PAIR):
            part = raw[:, low : low + PAIR]
            raw_ref[:, low : low + PAIR] = (
                part * cosine + swap_halves(part, half_size) * sine
            ).astype(jnp.bfloat16)
    v_ref[...] = (
        0.5 * forward_dot(normed, wv_ref[...]) + 0.5 * first_ref[...].astype(jnp.float32)
    ).astype(jnp.bfloat16)
    for bucket in range(bucket_count):
        base = bucket * slot_count
        for low in range(0, width, PAIR):
            keys = k_ref[base : base + slot_count, low : low + PAIR]
            queries = q_ref[base : base + slot_count, low : low + PAIR] * score_scale
            values_t = v_ref[base : base + slot_count, low : low + PAIR].T
            for start in range(0, slot_count, query_rows):
                end = start + query_rows
                parts = []
                for head in range(PAIR // head_size):
                    key_head = head_part(keys[:end], head, head_size)
                    scores = (
                        contract_last(key_head, queries[start:end])
                        + bias_ref[bucket, :end, start:end]
                    )
                    top = jnp.max(scores, axis=0, keepdims=True)
                    weights = jnp.exp(scores - top)
                    mass = jnp.sum(weights, axis=0, keepdims=True)
                    row = (low // head_size) + head
                    lse_ref[bucket, 0, row : row + 1, start:end] = top + jnp.log(mass)
                    mixed = forward_dot(
                        values_t[head * head_size : (head + 1) * head_size, :end],
                        weights.astype(jnp.bfloat16),
                    )
                    parts.append(mixed * (1.0 / mass))
                ctx_ref[base + start : base + end, low : low + PAIR] = (
                    jnp.concatenate(parts, axis=0).T.astype(jnp.bfloat16)
                )


def attend(normed, weights, first_values, bias, cosine, sine, head_size, width):
    token_count, model_width = normed.shape
    bucket_count, slot_count = bias.shape[:2]
    steps = model_width // width
    whole = lambda step: (0, 0)
    block = pl.BlockSpec((token_count, width), lambda step: (0, step))
    heads = width // head_size
    table = pl.BlockSpec((token_count, PAIR), whole)
    low_shape = jax.ShapeDtypeStruct((token_count, steps * width), jnp.bfloat16)
    return pl.pallas_call(
        partial(attend_kernel, slot_count, head_size),
        grid=(steps,),
        in_specs=[
            pl.BlockSpec((token_count, model_width), whole),
            pl.BlockSpec((model_width, width), lambda step: (0, step)),
            pl.BlockSpec((model_width, width), lambda step: (0, steps + step)),
            pl.BlockSpec((model_width, width), lambda step: (0, 2 * steps + step)),
            block,
            pl.BlockSpec((bucket_count, slot_count, slot_count), lambda step: (0, 0, 0)),
            table,
            table,
        ],
        out_specs=[
            block,
            block,
            block,
            block,
            pl.BlockSpec((bucket_count, 1, heads, slot_count), lambda step: (0, step, 0, 0)),
        ],
        out_shape=[low_shape] * 4
        + [jax.ShapeDtypeStruct((bucket_count, steps, heads, slot_count), jnp.float32)],
        compiler_params=pltpu.CompilerParams(vmem_limit_bytes=56 << 20),
        name="attend",
    )(normed, weights, weights, weights, first_values, bias, cosine, sine)


def attend_back_kernel(
    slot_count,
    head_size,
    q_ref,
    k_ref,
    v_ref,
    grad_ref,
    lse_ref,
    bias_ref,
    cos_ref,
    sin_ref,
    *rest,
):
    normed_t_ref = rest[0]
    grads_ref, first_ref, kept_ref, sent_ref, dk_ref, dv_ref = rest[-6:]
    half_size = head_size // 2
    score_scale = head_size ** (-0.5)
    width = q_ref.shape[1]
    bucket_count = bias_ref.shape[0]
    query_rows = slot_count // 2
    head_count = PAIR // head_size
    for bucket in range(bucket_count):
        base = bucket * slot_count
        cosine = cos_ref[base : base + slot_count]
        sine = sin_ref[base : base + slot_count]
        for low in range(0, width, PAIR):
            keys = k_ref[base : base + slot_count, low : low + PAIR]
            values = v_ref[base : base + slot_count, low : low + PAIR]
            queries = q_ref[base : base + slot_count, low : low + PAIR] * score_scale
            grads = grad_ref[base : base + slot_count, low : low + PAIR]
            keys_t = keys.T
            query_parts = []
            for start in range(0, slot_count, query_rows):
                end = start + query_rows
                parts = []
                for head in range(head_count):
                    row = (low // head_size) + head
                    scores = contract_last(
                        head_part(keys[:end], head, head_size), queries[start:end]
                    )
                    probs = jnp.exp(
                        scores
                        + bias_ref[bucket, :end, start:end]
                        - lse_ref[bucket, 0, row : row + 1, start:end]
                    )
                    grad_probs = contract_last(
                        head_part(values[:end], head, head_size), grads[start:end]
                    )
                    weighted = probs * grad_probs
                    grad_scores = (
                        weighted - probs * jnp.sum(weighted, axis=0, keepdims=True)
                    ).astype(jnp.bfloat16)
                    dv = forward_dot(probs.astype(jnp.bfloat16), grads[start:end])
                    dk = forward_dot(grad_scores, queries[start:end])
                    if start == 0:
                        dv_ref[head, :end] = dv
                        dk_ref[head, :end] = dk
                    else:
                        dv_ref[head, :start] += dv[:start]
                        dk_ref[head, :start] += dk[:start]
                        dv_ref[head, start:end] = dv[start:]
                        dk_ref[head, start:end] = dk[start:]
                    parts.append(
                        forward_dot(
                            keys_t[head * head_size : (head + 1) * head_size, :end], grad_scores
                        )
                    )
                query_parts.append((jnp.concatenate(parts, axis=0) * score_scale).T)
            lane = lax.broadcasted_iota(jnp.int32, (slot_count, PAIR), 1)
            dv = dv_ref[0]
            dk = dk_ref[0]
            for head in range(1, head_count):
                here = lane // head_size == head
                dv = jnp.where(here, dv_ref[head], dv)
                dk = jnp.where(here, dk_ref[head], dk)
            dq = jnp.concatenate(query_parts, axis=0)
            rows = slice(base, base + slot_count)
            for index, part in enumerate((dq, dk)):
                grads_ref[index, rows, low : low + PAIR] = (
                    part * cosine - swap_halves(part, half_size) * sine
                ).astype(jnp.bfloat16)
            first_ref[rows, low : low + PAIR] = 0.5 * dv
            grads_ref[2, rows, low : low + PAIR] = (0.5 * dv).astype(jnp.bfloat16)
    products = [(normed_t_ref, grads_ref.at[index]) for index in range(3)]
    if kept_ref.shape[0] > 3:
        products += [(rest[1], rest[2]), (rest[1], rest[3])]
    half = kept_ref.shape[1]
    for index, (left_ref, right_ref) in enumerate(products):
        right = right_ref[...]
        kept_ref[index] = forward_dot(left_ref[:half], right).astype(jnp.bfloat16)
        sent_ref[index] = forward_dot(left_ref[half:], right).astype(jnp.bfloat16)


def attend_back(
    queries,
    keys,
    values,
    grads,
    lse,
    bias,
    cosine,
    sine,
    normed_t,
    context_t,
    grad_hidden_low,
    head_size,
    width,
    first_step,
    steps,
    first,
):
    token_count, model_width = queries.shape
    bucket_count, slot_count = bias.shape[:2]
    heads = width // head_size
    block = pl.BlockSpec((token_count, width), lambda step: (0, first_step + step))
    table = pl.BlockSpec((token_count, PAIR), lambda step: (0, 0))
    lead = 3 if context_t is None else 5
    out_args = [] if context_t is None else [context_t, grad_hidden_low, grad_hidden_low]
    shared = [] if first is None else [first]
    return pl.pallas_call(
        partial(attend_back_kernel, slot_count, head_size),
        grid=(steps,),
        in_specs=[
            block,
            block,
            block,
            block,
            pl.BlockSpec(
                (bucket_count, 1, heads, slot_count), lambda step: (0, first_step + step, 0, 0)
            ),
            pl.BlockSpec((bucket_count, slot_count, slot_count), lambda step: (0, 0, 0)),
            table,
            table,
            pl.BlockSpec((model_width, token_count), lambda step: (0, 0)),
            pl.BlockSpec((model_width, token_count), lambda step: (0, 0)),
            pl.BlockSpec((token_count, width), lambda step: (0, step)),
            pl.BlockSpec((token_count, width), lambda step: (0, steps + step)),
        ][: 9 + len(out_args)]
        + [pl.BlockSpec(memory_space=pl.ANY)] * len(shared),
        out_specs=[
            pl.BlockSpec((3, token_count, width), lambda step: (0, 0, step)),
            block,
        ]
        + [pl.BlockSpec((lead, model_width // 2, width), lambda step: (0, 0, step))] * 2,
        out_shape=[
            jax.ShapeDtypeStruct((3, token_count, steps * width), jnp.bfloat16),
            jax.ShapeDtypeStruct((token_count, model_width), jnp.float32),
        ]
        + [jax.ShapeDtypeStruct((lead, model_width // 2, steps * width), jnp.bfloat16)] * 2,
        scratch_shapes=[
            pltpu.VMEM((PAIR // head_size, slot_count, PAIR), jnp.float32),
            pltpu.VMEM((PAIR // head_size, slot_count, PAIR), jnp.float32),
        ],
        input_output_aliases={9 + len(out_args): 1} if shared else {},
        compiler_params=pltpu.CompilerParams(vmem_limit_bytes=56 << 20),
        cost_estimate=pl.CostEstimate(flops=1, transcendentals=0, bytes_accessed=1),
        name="attend_back",
    )(queries, keys, values, grads, lse, bias, cosine, sine, normed_t, *out_args, *shared)


def feed_kernel(
    normed_ref,
    normed_t_ref,
    grad_y_ref,
    grad_product_ref,
    gate_ref,
    up_ref,
    product_ref,
    grad_gate_ref,
    grad_up_ref,
    gate_kept_ref,
    gate_sent_ref,
    up_kept_ref,
    up_sent_ref,
    down_ref,
):
    gate_values = forward_dot(normed_ref[...], gate_ref[...])
    upward = forward_dot(normed_ref[...], up_ref[...])
    grad_product = grad_product_ref[...]
    sigmoid_gate = jax.nn.sigmoid(gate_values)
    silu_gate = gate_values * sigmoid_gate
    product = (silu_gate * upward).astype(jnp.bfloat16)
    product_ref[...] = product
    grad_up_ref[...] = (grad_product * silu_gate).astype(jnp.bfloat16)
    grad_gate_ref[...] = (
        grad_product * upward * sigmoid_gate * (1.0 + gate_values * (1.0 - sigmoid_gate))
    ).astype(jnp.bfloat16)
    half = gate_kept_ref.shape[0]
    for grads_ref, kept_ref, sent_ref in (
        (grad_gate_ref, gate_kept_ref, gate_sent_ref),
        (grad_up_ref, up_kept_ref, up_sent_ref),
    ):
        grads = grads_ref[...]
        kept_ref[...] = forward_dot(normed_t_ref[:half], grads).astype(jnp.bfloat16)
        sent_ref[...] = forward_dot(normed_t_ref[half:], grads).astype(jnp.bfloat16)
    down_ref[...] = forward_dot(product.T, grad_y_ref[...]).astype(jnp.bfloat16)


def feed(normed, normed_t, grad_y, grad_product, weights):
    token_count, model_width = normed.shape
    hidden_width = grad_product.shape[1]
    width = 256
    steps = hidden_width // width
    whole = lambda step: (0, 0)
    wide = pl.BlockSpec((token_count, width), lambda step: (0, step))
    half = pl.BlockSpec((model_width // 2, width), lambda step: (0, step))
    wide_shape = jax.ShapeDtypeStruct((token_count, hidden_width), jnp.bfloat16)
    half_shape = jax.ShapeDtypeStruct((model_width // 2, hidden_width), jnp.bfloat16)
    return pl.pallas_call(
        feed_kernel,
        grid=(steps,),
        in_specs=[
            pl.BlockSpec((token_count, model_width), whole),
            pl.BlockSpec((model_width, token_count), whole),
            pl.BlockSpec((token_count, model_width), whole),
            wide,
            pl.BlockSpec((model_width, width), lambda step: (0, step)),
            pl.BlockSpec((model_width, width), lambda step: (0, steps + step)),
        ],
        out_specs=[wide] * 3
        + [half] * 4
        + [pl.BlockSpec((width, model_width), lambda step: (step, 0))],
        out_shape=[wide_shape] * 3
        + [half_shape] * 4
        + [jax.ShapeDtypeStruct((hidden_width, model_width), jnp.bfloat16)],
        compiler_params=pltpu.CompilerParams(vmem_limit_bytes=56 << 20),
        cost_estimate=pl.CostEstimate(flops=1, transcendentals=0, bytes_accessed=1),
        name="feed",
    )(normed, normed_t, grad_y, grad_product, weights, weights)


def finish_kernel(
    low_one_ref,
    low_two_ref,
    wq_ref,
    wk_ref,
    wv_ref,
    hidden_ref,
    x_ref,
    scale_ref,
    gain_ref,
    out_ref,
):
    half = low_one_ref.shape[2]
    total = None
    for index, w_ref in enumerate((wq_ref, wk_ref, wv_ref)):
        for low_ref, start in ((low_one_ref, 0), (low_two_ref, half)):
            part = contract_last(low_ref[index], w_ref[:, start : start + half])
            total = part if total is None else total + part
    inner = total * gain_ref[...]
    inputs = x_ref[...].astype(jnp.float32)
    scale = scale_ref[...]
    mean = jnp.mean(inner * inputs, axis=-1, keepdims=True)
    out_ref[...] = hidden_ref[...] + scale * inner - inputs * scale**3 * mean


def finish(low_one, low_two, weights, grad_hidden, inputs, scale, gain):
    token_count, model_width = inputs.shape
    rows = token_count // 4
    row_block = pl.BlockSpec((rows, model_width), lambda step: (step, 0))
    low_block = pl.BlockSpec((3, rows, model_width // 2), lambda step: (0, step, 0))
    weight_blocks = [
        pl.BlockSpec((model_width, model_width), lambda step, index=index: (0, index))
        for index in range(3)
    ]
    return pl.pallas_call(
        finish_kernel,
        grid=(4,),
        in_specs=[low_block, low_block]
        + weight_blocks
        + [
            row_block,
            row_block,
            pl.BlockSpec((rows, 1), lambda step: (step, 0)),
            pl.BlockSpec((1, model_width), lambda step: (0, 0)),
        ],
        out_specs=row_block,
        out_shape=jax.ShapeDtypeStruct((token_count, model_width), jnp.float32),
        compiler_params=pltpu.CompilerParams(vmem_limit_bytes=56 << 20),
        cost_estimate=pl.CostEstimate(flops=1, transcendentals=0, bytes_accessed=1),
        name="finish",
    )(low_one, low_two, weights, weights, weights, grad_hidden, inputs, scale, gain)


AXES = ("dp", "fsdp")


def flip(value, mask, device_count):
    pairs = [(place, place ^ mask) for place in range(device_count)]
    return lax.ppermute(value, AXES, pairs)


def masks_of(bits):
    masks = [0]
    for bit in bits:
        masks += [mask | 1 << bit for mask in masks]
    return masks


class Exchange:
    def __init__(self, partial_sum, steps, place, device_count, first=None):
        self.current = partial_sum
        self.first = first
        self.steps = [list(step) for step in steps]
        self.left = sorted([bit for step in steps for bit in step], reverse=True)
        self.place = place
        self.device_count = device_count
        self.got = None

    def part(self, mask):
        value = self.current
        left = list(self.left)
        for bit in self.steps[0]:
            lead, row_count, width = value.shape
            high = 1 << left.index(bit)
            view = value.reshape(lead, high, 2, row_count // (2 * high), width)
            chosen = ((self.place ^ mask) >> bit) & 1
            value = lax.dynamic_index_in_dim(view, chosen, 2, keepdims=False)
            value = value.reshape(lead, row_count // 2, width)
            left.remove(bit)
        return value

    def outgoing(self):
        if self.first is not None:
            self.kept, sent = self.first
            self.first = None
            return [sent]
        masks = masks_of(self.steps[0])
        self.kept = self.part(0)
        return [self.part(mask) for mask in masks[1:]]

    def launch(self, sent):
        masks = masks_of(self.steps[0])[1:]
        self.got = [flip(value, mask, self.device_count) for value, mask in zip(sent, masks)]

    def settle(self, got):
        total = self.kept.astype(jnp.float32)
        for value in got:
            total = total + value.astype(jnp.float32)
        for bit in self.steps.pop(0):
            self.left.remove(bit)
        self.current = total.astype(jnp.bfloat16) if self.steps else total


class Gather:
    def __init__(self, rows, steps, place, device_count):
        self.current = rows
        self.steps = [list(step) for step in steps]
        self.have = []
        self.place = place
        self.device_count = device_count
        self.got = None

    def outgoing(self):
        return [self.current]

    def launch(self, sent):
        masks = masks_of(self.steps[0])[1:]
        self.got = [flip(sent[0], mask, self.device_count) for mask in masks]

    def settle(self, got):
        pieces = [self.current] + list(got)
        for bit in self.steps.pop(0):
            row_count, width = pieces[0].shape
            high = 1 << len([other for other in self.have if other > bit])
            shape = (high, 1, row_count // high, width)
            side = lax.broadcasted_iota(jnp.int32, (1, 2, 1, 1), 1)
            mine = side == ((self.place >> bit) & 1)
            pieces = [
                jnp.where(mine, near.reshape(shape), far.reshape(shape)).reshape(
                    2 * row_count, width
                )
                for near, far in zip(pieces[0::2], pieces[1::2])
            ]
            self.have.append(bit)
        self.current = pieces[0]


def split_columns(matrix, bit, place, device_count):
    row_count, column_count = matrix.shape
    low = (column_count // device_count) << bit
    mine = (place >> bit) & 1
    return [
        jnp.concatenate(
            [
                lax.dynamic_slice(matrix, (0, start + side * low), (row_count, low))
                for start in range(0, column_count, 2 * low)
            ],
            axis=1,
        )
        for side in (mine, 1 - mine)
    ]


def tick(chain, settled, launched):
    settled = [item for item in settled if item.got is not None]
    if settled:
        chain, gots = lax.optimization_barrier((chain, [item.got for item in settled]))
        for item, got in zip(settled, gots):
            item.settle(got)
            item.got = None
    launched = [item for item in launched if item.steps and item.got is None]
    if launched:
        chain, sents = lax.optimization_barrier((chain, [item.outgoing() for item in launched]))
        for item, sent in zip(launched, sents):
            item.launch(sent)
    return chain


def step_plans(dp_size, fsdp_size):
    bit_count = (dp_size * fsdp_size).bit_length() - 1
    core_bit = fsdp_size.bit_length() - 1
    high = list(range(core_bit + 1, bit_count))
    rest = list(range(1, core_bit))
    pairs = [rest[index : index + 2] for index in range(0, len(rest), 2)]
    core = [core_bit]
    singles = [[bit] for bit in rest]
    return {
        "high_first": [core, high, [0]] + singles,
        "low_first": [core, [0], high] + singles,
        "tail": singles,
        "short": [core, high + [0]] + pairs,
        "gather": pairs[::-1] + [[0] + high, core],
    }


def shards(
    dp_size,
    fsdp_size,
    tokens,
    first_values,
    cotangent,
    lengths,
    w_query,
    w_key,
    w_value,
    w_out,
    w_gate,
    w_up,
    w_down,
    gain_one,
    gain_two,
):
    device_count = dp_size * fsdp_size
    place = lax.axis_index("dp") * fsdp_size + lax.axis_index("fsdp")
    plans = step_plans(dp_size, fsdp_size)
    micro_count = lengths.shape[0]
    token_count, model_width = tokens.shape
    slot_count = token_count // micro_count
    head_size = model_width // HEADS
    hidden_width = w_gate.shape[1]
    width = 4 * head_size
    half_width = model_width // 2
    half_steps = half_width // width
    exchange = partial(Exchange, place=place, device_count=device_count)

    gain_columns = jnp.pad(jnp.stack([gain_one, gain_two], axis=1), ((0, 0), (0, 126)))
    gather = partial(Gather, place=place, device_count=device_count)
    projections = (w_query, w_key, w_value)
    first_set = lax.all_gather(
        jnp.concatenate([*projections, gain_columns], axis=1), AXES, axis=0, tiled=True
    )
    second_set = lax.all_gather(
        jnp.concatenate([w_gate, w_up], axis=1), AXES, axis=0, tiled=True
    )
    out_rows = gather(w_out, plans["gather"])
    down_rows = gather(w_down, plans["gather"])

    inputs = tokens.astype(jnp.float32)
    layouts = [bucket_layout(lengths[index], slot_count) for index in range(micro_count)]
    position = jnp.concatenate([layout[1] for layout in layouts])
    valid = jnp.concatenate([layout[2] for layout in layouts])
    cosine, sine = rope_tables(position, head_size)
    cosine = jnp.tile(cosine, (1, 2 * PAIR // head_size))
    sine = jnp.tile(jnp.concatenate([-sine, sine], axis=1), (1, PAIR // head_size))
    bias = jnp.stack(
        [
            jnp.where(allowed_mask(layout[0], layout[2]).T, 0.0, -1e30).astype(jnp.float32)
            for layout in layouts
        ]
    )
    scale_one = rms_scale(inputs)

    scale_one, cosine, sine, bias = tick(
        (scale_one, cosine, sine, bias), [], [out_rows, down_rows]
    )
    scale_one, cosine, sine, bias = tick(
        (scale_one, cosine, sine, bias), [out_rows, down_rows], [out_rows]
    )
    scale_one = tick(scale_one, [out_rows], [])
    gain_first_f = first_set[:, 3 * model_width].astype(jnp.float32)[None, :]
    gain_second_f = first_set[:, 3 * model_width + 1].astype(jnp.float32)[None, :]
    normed = (inputs * scale_one * gain_first_f).astype(jnp.bfloat16)
    normed = tick(normed, [], [out_rows, down_rows])
    query_rot, key_rot, value_mix, context, lse = attend(
        normed, first_set, first_values, bias, cosine, sine, head_size, width
    )
    context = tick(context, [out_rows, down_rows], [out_rows, down_rows])
    while out_rows.steps:
        context = tick(context, [out_rows], [out_rows])
    out_w = out_rows.current
    hidden = inputs + forward_dot(context, out_w)
    scale_two = rms_scale(hidden)
    normed_two = (hidden * scale_two * gain_second_f).astype(jnp.bfloat16)
    gate_w = second_set[:, :hidden_width]
    up_w = second_set[:, hidden_width:]
    while down_rows.steps:
        normed_two = tick(normed_two, [down_rows], [down_rows])
    down_w = down_rows.current
    grad_y = cotangent.astype(jnp.float32) * valid.astype(jnp.float32)[:, None]
    grad_y_low = grad_y.astype(jnp.bfloat16)
    grad_product = contract_last(grad_y_low, down_w)
    core_bit = fsdp_size.bit_length() - 1
    normed_t, context_t, two_t = [
        jnp.concatenate(split_columns(matrix, core_bit, place, device_count), axis=1).T
        for matrix in (normed, context, normed_two)
    ]
    normed_two, grad_product, normed_t, context_t, two_t = lax.optimization_barrier(
        (normed_two, grad_product, normed_t, context_t, two_t)
    )
    product, grad_gate_low, grad_upward, *feed_parts = feed(
        normed_two, two_t, grad_y_low, grad_product, second_set
    )
    gate_parts, up_parts = [
        [part[None] for part in feed_parts[start : start + 2]] for start in (0, 2)
    ]
    gate = exchange(None, plans["low_first"], first=gate_parts)
    up = exchange(None, plans["high_first"], first=up_parts)
    down = exchange(feed_parts[4][None], plans["high_first"])
    grad_upward, grad_gate_low = tick((grad_upward, grad_gate_low), [], [gate, up, down])
    grad_normed_two = contract_last(grad_gate_low, gate_w) + contract_last(grad_upward, up_w)
    grad_normed_two = tick(grad_normed_two, [gate, up, down], [gate, up])
    inner_two = grad_normed_two * gain_second_f
    grad_hidden = (
        grad_y
        + scale_two * inner_two
        - hidden * scale_two**3 * jnp.mean(inner_two * hidden, axis=-1, keepdims=True)
    )
    grad_hidden_low = grad_hidden.astype(jnp.bfloat16)
    grad_context = contract_last(grad_hidden_low, out_w).astype(jnp.bfloat16)
    def attend_back_half(half, grad_context, first, outs):
        return attend_back(
            query_rot,
            key_rot,
            value_mix,
            grad_context,
            lse,
            bias,
            cosine,
            sine,
            normed_t,
            *outs,
            head_size,
            width,
            half * half_steps,
            half_steps,
            first,
        )

    low_one, first_part, *parts_one = attend_back_half(
        0, grad_context, None, (context_t, grad_hidden_low)
    )
    one = exchange(None, plans["low_first"], first=parts_one)
    grad_context, product = tick((grad_context, product), [gate, up], [gate, up, one])
    out_tokens = (hidden + forward_dot(product, down_w)).astype(jnp.bfloat16)
    grad_context, out_tokens = tick((grad_context, out_tokens), [gate, up, one], [])
    gate_up = exchange(
        jnp.concatenate([gate.current, up.current]), plans["tail"]
    )
    grad_context, out_tokens = tick((grad_context, out_tokens), [], [down, one, gate_up])
    low_two, grad_first, *parts_two = attend_back_half(1, grad_context, first_part, (None, None))
    two = exchange(None, plans["short"], first=parts_two)
    low_two = tick(low_two, [down, one, gate_up], [two, down, one, gate_up])
    grad_tokens = finish(
        low_one, low_two, first_set, grad_hidden, tokens, scale_one, gain_first_f
    )
    grad_tokens = tick(grad_tokens, [two, down, one, gate_up], [two, down, one])
    pending = [two, down, one, gate_up]
    while any(item.steps for item in pending):
        grad_tokens = tick(grad_tokens, pending, pending)
    projection_sums = [
        jnp.concatenate([one.current[index], two.current[index]], axis=1) for index in range(3)
    ]
    grad_out_sum = jnp.concatenate([one.current[3], one.current[4]], axis=1)
    grad_gate_sum = gate_up.current[0]
    grad_up_sum = gate_up.current[1]
    grad_down_sum = down.current[0]

    def gain_grad(gain, sums, weights):
        total = sum(
            jnp.sum(grads * weight.astype(jnp.float32), axis=1)
            for grads, weight in zip(sums, weights)
        )
        return total / gain.astype(jnp.float32)

    return (
        out_tokens,
        grad_tokens,
        grad_first,
        *projection_sums,
        grad_out_sum,
        grad_gate_sum,
        grad_up_sum,
        grad_down_sum,
        gain_grad(gain_one, projection_sums, projections),
        gain_grad(gain_two, (grad_gate_sum, grad_up_sum), (w_gate, w_up)),
    )


def solution(mesh):
    rows = P(AXES, None)
    ends = P(AXES)
    return jax.shard_map(
        partial(shards, mesh.shape["dp"], mesh.shape["fsdp"]),
        mesh=mesh,
        in_specs=(rows,) * 11 + (ends,) * 2,
        out_specs=(rows,) * 10 + (ends,) * 2,
        check_vma=False,
    )
```
